32 devices in a mesh: seq: 16 (over z, y, x), head: 2 (over core).
Axes of the slice: x: 2, y: 2, z: 4, core: 2. Of those that a mesh axis runs over, the one named last changes fastest.
Arguments:
- queries: bfloat16 [16384, 2048], P('seq', 'head'), may hold values from -5 to 5
- lin_keys: bfloat16 [16384, 2048], P('seq', 'head'), may hold values from -6 to 6
- lin_values: bfloat16 [16384, 2048], P('seq', 'head'), may hold values from -6 to 6
- window_keys: bfloat16 [16384, 512], P('seq', 'head'), may hold values from -5 to 5
- window_values: bfloat16 [16384, 512], P('seq', 'head'), may hold values from -6 to 6
- level_index: int32 [15, 16384], P(None, 'seq'), may hold values from 0 to 7
- level_table: float32 [8, 16], P(None, 'head'), may hold values from 0.25 to 2
- seq_lengths: int32 [4], replicated, may hold values from 1 to 8, 16 in all
- gain_linear: float32 [2048], P('head'), may hold values from 0.25 to 1.75
- gain_window: float32 [2048], P('head'), may hold values from 0.25 to 1.75
- w_out: bfloat16 [2048, 2048], P('head'), may hold values from -0.125 to 0.125
Outputs:
- mixed: bfloat16 [16384, 2048], P(('seq', 'head'))
The draws below stay inside these ranges and needn't reach their ends.
Inputs may be any that keep to these rules, and one draw needn't show every extreme that they name: `seq_lengths`: lengths of 4 consecutive sequences in whole shards of 1024 tokens, in order from token 0; they add up to the shards of seq and the longest has exactly half of them.
All inputs are finite; a program needn't handle non-finite values.
Results may differ from the reference program's by a relative error of at most 0.0095.
Values may be sent and summed in bfloat16 or wider, within the bound.
No kernel may reach another device: no remote copies, remote signals or barrier semaphores. Data moves between devices by JAX's collectives and lax.ppermute only.
A program may use at most 128 MiB of HBM per device.

```python
import math
import jax
import jax.numpy as jnp
import numpy as np
from jax import lax

DH = 128
HEADS = 16
KV_HEADS = 4
D = 2048
WINDOW = 256
BLOCK = 512
TABLE = 8
SEQS = 4
TOK_DEV = 1024
TOKENS = 16384
LEVELS = 15
N_SEQ = 16
N_HEAD = 2


def drawn_pair(key):
    base_key = jax.random.fold_in(key, 4242)
    key_one, key_two = jax.random.split(base_key, 2)
    queries = jnp.clip(jax.random.normal(key_one, (TOKENS, HEADS * DH), jnp.float32), -5.0, 5.0)
    keys_window = jnp.clip(jax.random.normal(key_two, (TOKENS, KV_HEADS * DH), jnp.float32), -5.0, 5.0)
    return (queries, keys_window)


def draw_queries(key, part):
    return drawn_pair(key)[0].astype(jnp.bfloat16)


def draw_window_keys(key, part):
    return drawn_pair(key)[1].astype(jnp.bfloat16)


def with_ends(result, own_key, smallest, largest):
    dims = result.shape
    spot = [jax.random.randint(jax.random.fold_in(own_key, axis), (), 0, dims[axis]) for axis in range(len(dims))]
    result = result.at[tuple(spot)].set(smallest)
    longest = dims.index(max(dims))
    spot[longest] = (spot[longest] + 1) % dims[longest]
    return result.at[tuple(spot)].set(largest)


def shard_levels(own_key, extent, cuts, low, top_value):
    loudness = 1.0
    for dim, blocks in cuts:
        steps = jax.random.uniform(jax.random.fold_in(jax.random.fold_in(own_key, 6), dim), (blocks,), jnp.float32, low / len(cuts), top_value / len(cuts))
        loudness = loudness * jnp.repeat(jnp.exp(steps), extent[dim] // blocks).reshape((-1,) + (1,) * (len(extent) - 1 - dim))
    return loudness


def split_up(number_of, total, bound, skew):
    loads = [(1 << 20) // math.isqrt(grade ** skew) + 1 for grade in range(2, number_of + 1)]
    rest, given = total - bound - (number_of - 1), [1] * (number_of - 1)
    while rest > 0:
        free = [i for i in range(number_of - 1) if given[i] < bound]
        mass, left = sum([loads[i] for i in free]), rest
        for i in free:
            addition = min(bound - given[i], max(1, left * loads[i] // mass), rest)
            given[i] = given[i] + addition
            rest = rest - addition
    return np.array([bound] + given)


def uneven(key, amount, total, limit, skew):
    if amount == 2:
        one = jax.random.randint(key, (), max(1, total - limit), min(limit, total - 1) + 1)
        return jnp.stack([one, total - one])
    tallies = jnp.asarray(split_up(amount, total, limit, skew), jnp.int32)
    twos = (amount - 1) // 2
    giver, taker = tallies[1:1 + 2 * twos:2], tallies[2:2 + 2 * twos:2]
    margin = jnp.minimum(giver - 1, limit - taker)
    shifted = jax.random.randint(jax.random.fold_in(key, 1), (twos,), 0, 1 << 20) % (margin + 1)
    tallies = tallies.at[1:1 + 2 * twos:2].set(giver - shifted).at[2:2 + 2 * twos:2].set(taker + shifted)
    return tallies[jax.random.permutation(jax.random.fold_in(key, 2), amount)]


def noise(stream_key, extent, deviation, bound, cuts=(), held_as=jnp.bfloat16):
    values = deviation * jax.random.normal(stream_key, extent, jnp.float32)
    if cuts:
        values = values * shard_levels(stream_key, extent, cuts, -0.22, 0.18)
    return jnp.clip(values, -bound, bound).astype(held_as)


def setup_inputs(seed: int = 0) -> dict:
    key_of = jax.random.split(jax.random.key(seed), 12)
    queries = draw_queries(jax.random.fold_in(key_of[11], 71), 0)
    lin_keys = noise(key_of[1], (TOKENS, HEADS * DH), 1.0, 6.0, ((0, 16), (1, 2)))
    lin_values = noise(key_of[2], (TOKENS, HEADS * DH), 1.0, 6.0, ((0, 16), (1, 2)))
    window_keys = draw_window_keys(jax.random.fold_in(key_of[11], 71), 0)
    window_values = noise(key_of[4], (TOKENS, KV_HEADS * DH), 1.0, 6.0, ((0, 16), (1, 2)))
    level_index = with_ends(jax.random.randint(key_of[5], (LEVELS, TOKENS), 0, TABLE), jax.random.fold_in(key_of[5], 1), 0, TABLE - 1).astype(jnp.int32)
    level_table = jnp.clip(jnp.exp(math.log(2.0) - 2.0794415 * jax.random.uniform(key_of[6], (TABLE, HEADS), jnp.float32) ** shard_levels(key_of[6], (TABLE, HEADS), ((1, 2),), -0.2, 0.2)), 0.25, 2.0)
    seq_lengths = uneven(key_of[7], SEQS, N_SEQ, N_SEQ // 2, 0).astype(jnp.int32)
    gain_linear = jnp.clip(1.0 + 0.15 * jax.random.normal(key_of[8], (HEADS * DH,), jnp.float32), 0.25, 1.75)
    gain_window = jnp.clip(1.0 + 0.15 * jax.random.normal(key_of[9], (HEADS * DH,), jnp.float32), 0.25, 1.75)
    w_out = noise(key_of[10], (HEADS * DH, D), (HEADS * DH) ** -0.5, 0.125, ((0, 2),))
    return {"queries": queries, "lin_keys": lin_keys, "lin_values": lin_values, "window_keys": window_keys, "window_values": window_values, "level_index": level_index, "level_table": level_table, "seq_lengths": seq_lengths, "gain_linear": gain_linear, "gain_window": gain_window, "w_out": w_out}


PRECISE = lax.Precision.HIGHEST
EPSILON = 1e-06

def bit_count(values, bit_width):
    running_total = jnp.zeros_like(values)
    for shift_by in range(bit_width):
        running_total = running_total + (values >= 1 << shift_by).astype(values.dtype)
    return running_total

def round_half(values):
    return lax.optimization_barrier(values.astype(jnp.bfloat16)).astype(jnp.float32)

def rms_scale(values, gain_vector):
    mean_square = lax.optimization_barrier(jnp.mean(values * values, axis=-1, keepdims=True))
    return values * lax.rsqrt(mean_square + EPSILON) * gain_vector

def level_weights(level_index, level_table):
    table_rows = jnp.arange(TABLE, dtype=jnp.int32)
    one_hot = (level_index[:, :, None] == table_rows[None, None, :]).astype(jnp.float32)
    level_scale = jnp.exp2(-0.5 * jnp.arange(LEVELS, dtype=jnp.float32))
    weights = jnp.einsum('ltk,kh->lth', one_hot, level_table.astype(jnp.float32), precision=PRECISE)
    return weights * level_scale[:, None, None]

def reference(queries, lin_keys, lin_values, window_keys, window_values, level_index, level_table, seq_lengths, gain_linear, gain_window, w_out):
    block_count = TOKENS // BLOCK
    block_bits = BLOCK.bit_length() - 1
    cross_levels = LEVELS - 1 - block_bits
    members = HEADS // KV_HEADS
    group_width = HEADS * DH // N_HEAD
    weights = level_weights(level_index, level_table)
    seq_ends = jnp.cumsum(seq_lengths)
    shard_ids = jnp.arange(N_SEQ, dtype=jnp.int32)
    shard_seq = lax.optimization_barrier(jnp.sum((shard_ids[:, None] >= seq_ends[None, :]).astype(jnp.int32), axis=1))
    block_seq = shard_seq[jnp.arange(block_count, dtype=jnp.int32) // (TOK_DEV // BLOCK)]
    query_heads = queries.reshape(TOKENS, HEADS, DH)
    key_heads = lin_keys.reshape(TOKENS, HEADS, DH)
    value_heads = lin_values.reshape(TOKENS, HEADS, DH)

    def block_state(pair_blocks):
        return jnp.einsum('shd,she->hde', pair_blocks[0].astype(jnp.float32), pair_blocks[1].astype(jnp.float32), precision=PRECISE)
    states = lax.map(block_state, (key_heads.reshape(block_count, BLOCK, HEADS, DH), value_heads.reshape(block_count, BLOCK, HEADS, DH)))
    offsets = jnp.arange(BLOCK, dtype=jnp.int32)
    level_grid = bit_count(jnp.bitwise_xor(offsets[:, None], offsets[None, :]), block_bits)
    causal = offsets[None, :] <= offsets[:, None]
    padded_keys = jnp.concatenate([jnp.zeros((WINDOW, KV_HEADS, DH), window_keys.dtype), window_keys.reshape(TOKENS, KV_HEADS, DH)], axis=0)
    padded_values = jnp.concatenate([jnp.zeros((WINDOW, KV_HEADS, DH), window_values.dtype), window_values.reshape(TOKENS, KV_HEADS, DH)], axis=0)
    linear_gain = gain_linear.reshape(HEADS, DH)
    window_gain = gain_window.reshape(HEADS, DH)

    def one_block(block_id):
        first_row = block_id * BLOCK
        query_block = lax.dynamic_slice_in_dim(query_heads, first_row, BLOCK, 0).astype(jnp.float32)
        key_block = lax.dynamic_slice_in_dim(key_heads, first_row, BLOCK, 0).astype(jnp.float32)
        value_block = lax.dynamic_slice_in_dim(value_heads, first_row, BLOCK, 0).astype(jnp.float32)
        weight_block = lax.dynamic_slice_in_dim(weights, first_row, BLOCK, 1)
        scores = jnp.einsum('thd,shd->hts', query_block, key_block, precision=PRECISE)
        mixing = jnp.zeros((HEADS, BLOCK, BLOCK), jnp.float32)
        for level_id in range(block_bits + 1):
            mixing = mixing + jnp.where(level_grid == level_id, 1.0, 0.0)[None, :, :] * weight_block[level_id].T[:, :, None]
        mixing = jnp.where(causal[None, :, :], mixing, 0.0)
        near_part = jnp.einsum('hts,shd->thd', round_half(scores * mixing), value_block, precision=PRECISE)
        far_part = jnp.zeros((BLOCK, HEADS, DH), jnp.float32)
        own_seq = block_seq[block_id]
        for bit_number in range(cross_levels):
            group_span = 1 << bit_number
            upper_edge = block_id // group_span * group_span
            lower_edge = jnp.maximum(upper_edge - group_span, 0).astype(jnp.int32)
            group_states = lax.dynamic_slice_in_dim(states, lower_edge, group_span, 0)
            group_seq = lax.dynamic_slice_in_dim(block_seq, lower_edge, group_span, 0)
            keep_mask = (group_seq == own_seq).astype(jnp.float32)
            bucket = jnp.einsum('j,jhde->hde', keep_mask, group_states, precision=PRECISE)
            present = (block_id // group_span % 2).astype(jnp.float32)
            reached = jnp.einsum('thd,hde->the', query_block, bucket, precision=PRECISE)
            far_part = far_part + present * weight_block[block_bits + 1 + bit_number][:, :, None] * reached
        linear_part = rms_scale(near_part + far_part, linear_gain)
        key_window = lax.dynamic_slice_in_dim(padded_keys, first_row, BLOCK + WINDOW, 0).astype(jnp.float32)
        value_window = lax.dynamic_slice_in_dim(padded_values, first_row, BLOCK + WINDOW, 0).astype(jnp.float32)
        key_pos = first_row - WINDOW + jnp.arange(BLOCK + WINDOW, dtype=jnp.int32)
        query_pos = first_row + offsets
        key_seq = shard_seq[jnp.maximum(key_pos, 0) // TOK_DEV]
        query_seq = shard_seq[query_pos // TOK_DEV]
        allowed = (key_pos[None, :] <= query_pos[:, None]) & (key_pos[None, :] > query_pos[:, None] - WINDOW) & (key_pos[None, :] >= 0) & (key_seq[None, :] == query_seq[:, None])
        grouped = query_block.reshape(BLOCK, KV_HEADS, members, DH)
        logits = jnp.einsum('tkgd,skd->kgts', grouped, key_window, precision=PRECISE) * DH ** (-0.5)
        logits = jnp.where(allowed[None, None, :, :], logits, -1e+30)
        row_peak = lax.optimization_barrier(jnp.max(logits, axis=-1, keepdims=True))
        exponents = jnp.exp(logits - row_peak)
        window_weights = round_half(exponents / lax.optimization_barrier(jnp.sum(exponents, axis=-1, keepdims=True)))
        window_raw = jnp.einsum('kgts,skd->tkgd', window_weights, value_window, precision=PRECISE).reshape(BLOCK, HEADS, DH)
        window_part = rms_scale(window_raw, window_gain)
        attended = (linear_part + window_part).astype(jnp.bfloat16).reshape(BLOCK, HEADS * DH)
        mixed_rows = jnp.zeros((BLOCK, D), jnp.float32)
        for member in range(N_HEAD):
            partial_sum = jnp.dot(attended[:, member * group_width:(member + 1) * group_width], w_out[member * group_width:(member + 1) * group_width], preferred_element_type=jnp.float32)
            mixed_rows = mixed_rows + round_half(partial_sum)
        return mixed_rows.astype(jnp.bfloat16)
    output_blocks = lax.map(one_block, jnp.arange(block_count, dtype=jnp.int32))
    return output_blocks.reshape(TOKENS, D)
```

```python
import functools

import jax
import jax.numpy as jnp
from jax import lax
from jax.experimental import pallas as pl
from jax.experimental.pallas import tpu as pltpu
from jax.sharding import PartitionSpec as P

DH = 128
WINDOW = 256
BLOCK = 512
NEAR = 256
TILE = 128
GROUP = 8
EPSILON = 1e-06
LOG2_E = 1.4426950408889634
BF16 = jnp.bfloat16
F32 = jnp.float32


def dot(a, b):
    return lax.dot_general(a, b, (((1,), (0,)), ((), ())), preferred_element_type=F32)


def dot_nt(a, b):
    return lax.dot_general(a, b, (((1,), (1,)), ((), ())), preferred_element_type=F32)


def local_buckets(tokens):
    blocks = tokens // NEAR
    found = []
    span = 1
    while span < blocks:
        for group in range(1, blocks // span, 2):
            found.append((span, group))
        span *= 2
    return found


def weight_rows(index, table_ref, head, first_level):
    rows = jnp.zeros(index.shape, F32)
    for k in range(table_ref.shape[0]):
        rows = jnp.where(index == k, table_ref[k, head], rows)
    level = lax.broadcasted_iota(jnp.int32, index.shape, 0) + first_level
    return rows * jnp.exp2(-0.5 * level.astype(F32))


def gain_columns(gain_ref):
    return jnp.broadcast_to(gain_ref[0], (DH, DH)).T


def state_kernel(k_ref, v_ref, vt_ref, local_ref, total_ref):
    tokens = k_ref.shape[0]
    blocks = tokens // NEAR
    values_t = v_ref[...].T
    vt_ref[...] = values_t
    states = [
        dot(values_t[:, b * NEAR : (b + 1) * NEAR], k_ref[b * NEAR : (b + 1) * NEAR, :])
        for b in range(blocks)
    ]
    for place, (span, group) in enumerate(local_buckets(tokens)):
        members = states[(group - 1) * span : group * span]
        local_ref[place] = functools.reduce(jnp.add, members).astype(BF16)
    total_ref[...] = functools.reduce(jnp.add, states).astype(BF16)


def tile_mixing(weights):
    shape = (GROUP, TILE)
    row = lax.broadcasted_iota(jnp.int32, shape, 0)
    lane = lax.broadcasted_iota(jnp.int32, shape, 1)
    inner_bits = GROUP.bit_length() - 1
    within = lane % GROUP
    differ = row ^ within
    inner = jnp.where(differ == 0, weights[0:1], 0.0)
    for bit in range(inner_bits):
        inner = jnp.where((differ >> bit == 1) & (row < within), weights[bit + 1 : bit + 2], inner)
    shape = (TILE // GROUP, TILE)
    row = lax.broadcasted_iota(jnp.int32, shape, 0)
    above = lax.broadcasted_iota(jnp.int32, shape, 1) // GROUP
    differ = row ^ above
    outer = jnp.zeros(shape, F32)
    for bit in range((TILE // GROUP).bit_length() - 1):
        level = inner_bits + 1 + bit
        outer = jnp.where((differ >> bit == 1) & (row < above), weights[level : level + 1], outer)
    pieces = [
        jnp.where(lane // GROUP == g, inner, jnp.broadcast_to(outer[g : g + 1], (GROUP, TILE)))
        for g in range(TILE // GROUP)
    ]
    return jnp.concatenate(pieces, axis=0)


def near_kernel(table_ref, index_ref, q_ref, k_ref, vt_ref, local_ref, out_ref):
    tokens = q_ref.shape[0]
    buckets = local_buckets(tokens)
    weights = weight_rows(index_ref[...], table_ref, pl.program_id(0), 0)
    near_bits = NEAR.bit_length() - 1
    for b in range(tokens // NEAR):
        at = slice(b * NEAR, (b + 1) * NEAR)
        queries = q_ref[at, :]
        scores = dot_nt(k_ref[at, :], queries)
        w_block = weights[:, at]
        low = scores[:TILE, :TILE] * tile_mixing(w_block[:, :TILE])
        cross = scores[:TILE, TILE:] * w_block[near_bits : near_bits + 1, TILE:]
        high = scores[TILE:, TILE:] * tile_mixing(w_block[:, TILE:])
        mixed = jnp.concatenate(
            [
                jnp.concatenate([low.astype(BF16), cross.astype(BF16)], axis=1),
                jnp.concatenate([jnp.zeros((TILE, TILE), BF16), high.astype(BF16)], axis=1),
            ],
            axis=0,
        )
        part = dot(vt_ref[:, at], mixed)
        for place, (span, group) in enumerate(buckets):
            if b // span == group:
                level = near_bits + 1 + span.bit_length() - 1
                part = part + dot_nt(local_ref[place], queries) * w_block[level : level + 1]
        out_ref[:, at] = part


def window_kernel(bias_ref, q_ref, k_ref, v_ref, rim_k_ref, rim_v_ref, gain_ref, out_ref, ext_k, ext_vt):
    tokens = k_ref.shape[0]
    pairs = q_ref.shape[1] // DH
    scale = LOG2_E * DH**-0.5

    @pl.when(pl.program_id(1) == 0)
    def _():
        ext_k[:WINDOW, :] = rim_k_ref[...]
        ext_k[WINDOW:, :] = k_ref[...]
        ext_vt[:, :WINDOW] = rim_v_ref[...].T
        ext_vt[:, WINDOW:] = v_ref[...].T

    bias = bias_ref[0]
    key_row = lax.broadcasted_iota(jnp.int32, (TILE, TILE * pairs), 0)
    query_lane = lax.broadcasted_iota(jnp.int32, (TILE, TILE * pairs), 1) % TILE
    causal = key_row <= query_lane
    gains = [jnp.broadcast_to(gain_ref[:, p * DH : (p + 1) * DH], (DH, DH)).T for p in range(pairs)]
    gain = jnp.concatenate(gains, axis=1)
    zero = jnp.zeros((), BF16)
    for b in range(tokens // TILE):
        at = slice(b * TILE, (b + 1) * TILE)
        queries = jnp.concatenate([q_ref[at, p * DH : (p + 1) * DH] for p in range(pairs)], axis=0)
        scores = dot_nt(ext_k[b * TILE : b * TILE + WINDOW + TILE, :], queries)
        oldest, middle, newest = scores[:TILE], scores[TILE : 2 * TILE], scores[2 * TILE :]
        if b * TILE < WINDOW:
            oldest = oldest + bias
        if (b + 1) * TILE < WINDOW:
            middle = middle + bias
        edge = jnp.where(causal, newest, oldest)
        peak = jnp.max(jnp.maximum(edge, middle), axis=0, keepdims=True)
        edge = jnp.exp2((edge - peak) * scale)
        middle = jnp.exp2((middle - peak) * scale)
        total = jnp.sum(edge + middle, axis=0, keepdims=True)
        edge = edge.astype(BF16)
        probs = jnp.concatenate(
            [jnp.where(causal, zero, edge), middle.astype(BF16), jnp.where(causal, edge, zero)], axis=0
        )
        raw = dot(ext_vt[:, b * TILE : b * TILE + WINDOW + TILE], probs)
        mean = jnp.sum(raw * raw, axis=0, keepdims=True) * (1.0 / DH)
        raw = (raw * lax.rsqrt(mean + EPSILON * total * total) * gain).astype(BF16)
        for p in range(pairs):
            out_ref[p * DH : (p + 1) * DH, at] = raw[:, p * TILE : (p + 1) * TILE]


def final_kernel(
    row_ref, mask_ref, table_ref, index_ref, q_ref, near_ref, win_ref, gain_ref, *rest, levels, has_added
):
    bucket_refs = rest[:levels]
    w_ref = rest[levels]
    added_ref = rest[levels + 1] if has_added else None
    out_ref, att, weights_out, sem = rest[levels + 1 + int(has_added) :]
    head = pl.program_id(0)
    copy = pltpu.make_async_copy(w_ref, weights_out, sem)

    @pl.when(head == 0)
    def _():
        copy.start()

    rows = q_ref.shape[0]
    first = index_ref.shape[0] - levels
    weights = weight_rows(index_ref[first:, :], table_ref, head, first)
    stacked = jnp.concatenate([ref[...] for ref in bucket_refs], axis=0)
    reached = dot_nt(stacked, q_ref[...])
    total = near_ref[...].astype(F32)
    for level in range(levels):
        total = total + reached[level * DH : (level + 1) * DH] * (
            weights[level : level + 1] * mask_ref[level]
        )
    mean = jnp.sum(total * total, axis=0, keepdims=True) * (1.0 / DH)
    gain = jnp.concatenate([gain_columns(gain_ref)] * (rows // DH), axis=1)
    total = total * lax.rsqrt(mean + EPSILON) * gain
    att[head] = (total + win_ref[...].astype(F32)).astype(BF16).T

    @pl.when(head == pl.num_programs(0) - 1)
    def _():
        copy.wait()
        heads = att.shape[0]
        attended = jnp.concatenate([att[h] for h in range(heads)], axis=1)
        columns = w_ref.shape[1]
        step = min(columns, 256)
        for c in range(0, columns, step):
            product = dot(attended, weights_out[:, c : c + step])
            if has_added:
                product = product + added_ref[:, c : c + step].astype(F32)
            out_ref[:, c : c + step] = product.astype(BF16)


def whole(shape):
    return pl.BlockSpec(shape, lambda *_: (0,) * len(shape))


SMEM = pl.BlockSpec(memory_space=pltpu.SMEM)


def make_shards(seq_count, head_count):
    def shards(
        queries,
        lin_keys,
        lin_values,
        window_keys,
        window_values,
        level_index,
        level_table,
        seq_lengths,
        gain_linear,
        gain_window,
        w_out,
    ):
        tokens = queries.shape[0]
        heads = level_table.shape[1]
        groups = window_keys.shape[1] // DH
        members = heads // groups
        pairs = 2 if members % 2 == 0 else 1
        levels = seq_count.bit_length() - 1
        buckets = len(local_buckets(tokens))
        shard = lax.axis_index("seq")

        starts = [jnp.int32(0)]
        for s in range(seq_lengths.shape[0] - 1):
            starts.append(starts[-1] + seq_lengths[s])

        def begin_of(index):
            begin = jnp.zeros_like(index)
            for start in starts[1:]:
                begin = jnp.where(start <= index, start, begin)
            return begin

        rim = jnp.concatenate([window_keys[tokens - WINDOW :], window_values[tokens - WINDOW :]], axis=1)
        rim = lax.ppermute(rim, "seq", [(i, (i + 1) % seq_count) for i in range(seq_count)])

        column = pl.BlockSpec((tokens, DH), lambda h: (0, h))
        row = pl.BlockSpec((DH, tokens), lambda h: (h, 0))
        values_t, local_states, state = pl.pallas_call(
            state_kernel,
            grid=(heads,),
            in_specs=[column, column],
            out_specs=[
                row,
                pl.BlockSpec((None, buckets, DH, DH), lambda h: (h, 0, 0, 0)),
                pl.BlockSpec((DH, DH), lambda h: (h, 0)),
            ],
            out_shape=[
                jax.ShapeDtypeStruct((heads * DH, tokens), BF16),
                jax.ShapeDtypeStruct((heads, buckets, DH, DH), BF16),
                jax.ShapeDtypeStruct((heads * DH, DH), BF16),
            ],
            name="states",
        )(lin_keys, lin_values)

        received = []
        for level in range(levels):
            arrived = lax.ppermute(state, "seq", [(i, i ^ (1 << level)) for i in range(seq_count)])
            received.append(arrived)
            if level < levels - 1:
                last = shard | ((2 << level) - 1)
                middle = last - (1 << level)
                joined = (begin_of(last) <= middle).astype(F32)
                right = (shard >> level) % 2 == 1
                own = jnp.where(right, 1.0, joined)
                other = jnp.where(right, joined, 1.0)
                state = (state.astype(F32) * own + arrived.astype(F32) * other).astype(BF16)

        level_ids = jnp.arange(levels, dtype=jnp.int32)
        bit_set = (shard >> level_ids) % 2 == 1
        below = ((shard >> level_ids) << level_ids) - 1
        begin = begin_of(shard)
        mask = (bit_set & (begin <= below)).astype(F32)
        bias = jnp.where(begin == shard, -1e30, 0.0).reshape(1).astype(F32)

        near = pl.pallas_call(
            near_kernel,
            grid=(heads,),
            in_specs=[
                SMEM,
                whole(level_index.shape),
                column,
                column,
                row,
                pl.BlockSpec((None, buckets, DH, DH), lambda h: (h, 0, 0, 0)),
            ],
            out_specs=row,
            out_shape=jax.ShapeDtypeStruct((heads * DH, tokens), F32),
            name="near",
        )(level_table, level_index, queries, lin_keys, values_t, local_states)

        per_group = members // pairs
        windowed = pl.pallas_call(
            window_kernel,
            grid=(groups, per_group),
            in_specs=[
                SMEM,
                pl.BlockSpec((tokens, pairs * DH), lambda g, p: (0, g * per_group + p)),
                pl.BlockSpec((tokens, DH), lambda g, p: (0, g)),
                pl.BlockSpec((tokens, DH), lambda g, p: (0, g)),
                pl.BlockSpec((WINDOW, DH), lambda g, p: (0, g)),
                pl.BlockSpec((WINDOW, DH), lambda g, p: (0, g + groups)),
                pl.BlockSpec((1, pairs * DH), lambda g, p: (0, g * per_group + p)),
            ],
            out_specs=pl.BlockSpec((pairs * DH, tokens), lambda g, p: (g * per_group + p, 0)),
            out_shape=jax.ShapeDtypeStruct((heads * DH, tokens), BF16),
            scratch_shapes=[
                pltpu.VMEM((tokens + WINDOW, DH), BF16),
                pltpu.VMEM((DH, tokens + WINDOW), BF16),
            ],
            name="window",
        )(bias, queries, window_keys, window_values, rim, rim, gain_window.reshape(1, heads * DH))

        rows = tokens // head_count
        width = w_out.shape[1]
        gain_rows = gain_linear.reshape(heads, 1, DH)

        def finish(block, added):
            has_added = added is not None
            bucket = pl.BlockSpec((DH, DH), lambda h, r: (h, 0))
            specs = [
                SMEM,
                SMEM,
                pl.BlockSpec((level_index.shape[0], rows), lambda h, r: (0, r[0])),
                pl.BlockSpec((rows, DH), lambda h, r: (r[0], h)),
                pl.BlockSpec((DH, rows), lambda h, r: (h, r[0])),
                pl.BlockSpec((DH, rows), lambda h, r: (h, r[0])),
                pl.BlockSpec((1, 1, DH), lambda h, r: (h, 0, 0)),
            ]
            specs += [bucket] * levels
            specs += [pl.BlockSpec(memory_space=pl.ANY)]
            operands = [mask, level_table, level_index, queries, near, windowed, gain_rows]
            operands += received + [w_out]
            if has_added:
                specs.append(pl.BlockSpec((rows, width), lambda h, r: (0, 0)))
                operands.append(added)
            return pl.pallas_call(
                functools.partial(final_kernel, levels=levels, has_added=has_added),
                grid_spec=pltpu.PrefetchScalarGridSpec(
                    num_scalar_prefetch=1,
                    grid=(heads,),
                    in_specs=specs,
                    out_specs=pl.BlockSpec((rows, width), lambda h, r: (0, 0)),
                    scratch_shapes=[
                        pltpu.VMEM((heads, rows, DH), BF16),
                        pltpu.VMEM(w_out.shape, BF16),
                        pltpu.SemaphoreType.DMA,
                    ],
                ),
                out_shape=jax.ShapeDtypeStruct((rows, width), BF16),
                name="final",
            )(block.reshape(1), *operands)

        place = lax.axis_index("head")
        arrived = []
        for away in range(1, head_count):
            partial = finish((place + away) % head_count, None)
            arrived.append(
                lax.ppermute(partial, "head", [(i, (i + away) % head_count) for i in range(head_count)])
            )
        own = finish(place, None)
        total = own.astype(F32)
        for part in arrived:
            total = total + part.astype(F32)
        return total.astype(BF16)

    return shards


def solution(mesh):
    placed = (
        P("seq", "head"),
        P("seq", "head"),
        P("seq", "head"),
        P("seq", "head"),
        P("seq", "head"),
        P(None, "seq"),
        P(None, "head"),
        P(),
        P("head"),
        P("head"),
        P("head", None),
    )
    return jax.shard_map(
        make_shards(mesh.shape["seq"], mesh.shape["head"]),
        mesh=mesh,
        in_specs=placed,
        out_specs=P(("seq", "head"), None),
        check_vma=False,
    )
```

```python
import functools

import jax
import jax.numpy as jnp
from jax import lax
from jax.experimental import pallas as pl
from jax.experimental.pallas import tpu as pltpu
from jax.sharding import PartitionSpec as P

DH = 128
WINDOW = 256
BLOCK = 512
NEAR = 256
TILE = 128
GROUP = 8
EPSILON = 1e-06
LOG2_E = 1.4426950408889634
MEGABYTE = 1 << 20
BF16 = jnp.bfloat16
F32 = jnp.float32


def dot(a, b):
    return lax.dot_general(a, b, (((1,), (0,)), ((), ())), preferred_element_type=F32)


def dot_nt(a, b):
    return lax.dot_general(a, b, (((1,), (1,)), ((), ())), preferred_element_type=F32)


def local_spans(tokens):
    spans = []
    span = 1
    while span < tokens // NEAR:
        spans.append(span)
        span *= 2
    return spans


def local_buckets(tokens):
    blocks = tokens // NEAR
    return [(span, group) for span in local_spans(tokens) for group in range(1, blocks // span, 2)]


def weight_rows(index, table_ref, head, first_level):
    rows = jnp.zeros(index.shape, F32)
    for k in range(table_ref.shape[0]):
        rows = jnp.where(index == k, table_ref[k, head], rows)
    level = lax.broadcasted_iota(jnp.int32, index.shape, 0) + first_level
    return rows * jnp.exp2(-0.5 * level.astype(F32))


def head_columns(h):
    return slice(h * DH, (h + 1) * DH)


def state_kernel(
    lengths_ref, k_hbm, v_hbm, k_ref, v_ref, local_ref, total_ref, flags_ref, states, sems, *, levels
):
    blocks = states.shape[0]
    heads = k_ref.shape[1] // DH
    copies = []
    for b in range(blocks):
        rows = pl.ds(b * NEAR, NEAR)
        pair = [
            pltpu.make_async_copy(k_hbm.at[rows], k_ref.at[rows], sems.at[0, b]),
            pltpu.make_async_copy(v_hbm.at[rows], v_ref.at[rows], sems.at[1, b]),
        ]
        for copy in pair:
            copy.start()
        copies.append(pair)
    for b in range(blocks):
        rows = slice(b * NEAR, (b + 1) * NEAR)
        for copy in copies[b]:
            copy.wait()
        for h in range(heads):
            at = head_columns(h)
            states[b, at, :] = dot(v_ref[rows, at].T, k_ref[rows, at])
    for place, (span, group) in enumerate(local_buckets(blocks * NEAR)):
        members = [states[b] for b in range((group - 1) * span, group * span)]
        local_ref[place] = functools.reduce(jnp.add, members).astype(BF16)
    total_ref[...] = functools.reduce(jnp.add, [states[b] for b in range(blocks)]).astype(BF16)

    shard = lax.axis_index("seq")
    starts = [jnp.int32(0)]
    for s in range(lengths_ref.shape[0] - 1):
        starts.append(starts[-1] + lengths_ref[s])

    def begin_of(index):
        begin = jnp.int32(0)
        for start in starts[1:]:
            begin = jnp.where(start <= index, start, begin)
        return begin

    begin = begin_of(shard)
    for level in range(levels):
        last = shard | ((2 << level) - 1)
        middle = last - (1 << level)
        joined = jnp.where(begin_of(last) <= middle, 1.0, 0.0)
        right = (shard & (1 << level)) != 0
        flags_ref[0, level] = jnp.where(right, 1.0, joined)
        flags_ref[1, level] = jnp.where(right, joined, 1.0)
        flags_ref[2, level] = jnp.where(right & (begin <= middle), 1.0, 0.0)
    for row in range(3):
        flags_ref[row, levels] = jnp.where(begin == shard, -1e30, 0.0)


def join_kernel(flags_ref, own_ref, arrived_ref, *rest, level):
    own, arrived = own_ref[...].astype(F32), arrived_ref[...].astype(F32)
    rest[-1][...] = (own * flags_ref[0, level] + arrived * flags_ref[1, level]).astype(BF16)


def tile_mixing(weights):
    shape = (GROUP, TILE)
    row = lax.broadcasted_iota(jnp.int32, shape, 0)
    lane = lax.broadcasted_iota(jnp.int32, shape, 1)
    inner_bits = GROUP.bit_length() - 1
    within = lane % GROUP
    differ = row ^ within
    inner = jnp.where(differ == 0, weights[0:1], 0.0)
    for bit in range(inner_bits):
        inner = jnp.where((differ >> bit == 1) & (row < within), weights[bit + 1 : bit + 2], inner)
    shape = (TILE // GROUP, TILE)
    row = lax.broadcasted_iota(jnp.int32, shape, 0)
    above = lax.broadcasted_iota(jnp.int32, shape, 1) // GROUP
    differ = row ^ above
    outer = jnp.zeros(shape, F32)
    for bit in range((TILE // GROUP).bit_length() - 1):
        level = inner_bits + 1 + bit
        outer = jnp.where((differ >> bit == 1) & (row < above), weights[level : level + 1], outer)
    pieces = [
        jnp.where(lane // GROUP == g, inner, jnp.broadcast_to(outer[g : g + 1], (GROUP, TILE)))
        for g in range(TILE // GROUP)
    ]
    return jnp.concatenate(pieces, axis=0)


def near_kernel(table_ref, index_ref, q_ref, k_ref, v_ref, local_ref, *rest, spans, start):
    out_ref = rest[-1]
    block = start + pl.program_id(0)
    blocks, width, _ = out_ref.shape
    near_bits = NEAR.bit_length() - 1
    tokens = pl.ds(pl.multiple_of(block * NEAR, NEAR), NEAR)
    index = index_ref[:, tokens]
    places, present = [], []
    first = 0
    for span in spans:
        group = block // span
        places.append(first + group // 2)
        present.append((group % 2).astype(F32))
        first += blocks // span // 2
    for h in range(width // DH):
        at = head_columns(h)
        weights = weight_rows(index, table_ref, h, 0)
        queries_t = q_ref[tokens, at].T
        scores = dot(k_ref[tokens, at], queries_t)
        low = scores[:TILE, :TILE] * tile_mixing(weights[:, :TILE])
        cross = scores[:TILE, TILE:] * weights[near_bits : near_bits + 1, TILE:]
        high = scores[TILE:, TILE:] * tile_mixing(weights[:, TILE:])
        lhs = [v_ref[tokens, at].T]
        rhs = [
            jnp.concatenate([low.astype(BF16), cross.astype(BF16)], axis=1),
            jnp.concatenate([jnp.zeros((TILE, TILE), BF16), high.astype(BF16)], axis=1),
        ]
        for i, place in enumerate(places):
            level = near_bits + 1 + i
            row = (weights[level : level + 1] * present[i]).astype(BF16)
            lhs.append(local_ref[place, at, :])
            rhs.append(queries_t * row)
        out_ref[block, at, :] = dot(jnp.concatenate(lhs, axis=1), jnp.concatenate(rhs, axis=0))


def gain_column(gain_ref, h):
    return jnp.broadcast_to(gain_ref[h], (DH, DH)).T


def window_kernel(flags_ref, q_ref, k_ref, v_ref, gain_ref, *rest, has_rim, members, start):
    out_ref, gains = rest[-2:]
    block = start + pl.program_id(0)
    heads = q_ref.shape[1] // DH
    scale = LOG2_E * DH**-0.5

    @pl.when(pl.program_id(0) == 0)
    def _():
        for h in range(heads):
            gains[h] = gain_column(gain_ref, h)

    key_row = lax.broadcasted_iota(jnp.int32, (TILE, TILE), 0)
    query_lane = lax.broadcasted_iota(jnp.int32, (TILE, TILE), 1)
    causal = key_row <= query_lane
    lower = jnp.where(causal, 1.0, 0.0).astype(BF16)
    now = pl.multiple_of(block * NEAR, NEAR)
    if has_rim:
        bias = flags_ref[0, flags_ref.shape[1] - 1]
    for g in range(heads // members):
        at = head_columns(g)
        if has_rim:
            rim_ref = rest[0]
            old_k = rim_ref[:, at]
            old_v = rim_ref[:, head_columns(g + heads // members)]
        else:
            old_k = k_ref[pl.ds(now - WINDOW, WINDOW), at]
            old_v = v_ref[pl.ds(now - WINDOW, WINDOW), at]
        keys = jnp.concatenate([old_k, k_ref[pl.ds(now, NEAR), at]], axis=0)
        values_t = jnp.concatenate([old_v.T, v_ref[pl.ds(now, NEAR), at].T], axis=1)
        for h in range(g * members, (g + 1) * members):
            for tile in range(NEAR // TILE):
                queries = q_ref[pl.ds(now + tile * TILE, TILE), head_columns(h)]
                span = slice(tile * TILE, tile * TILE + WINDOW + TILE)
                scores = dot_nt(keys[span], queries)
                oldest, middle, newest = scores[:TILE], scores[TILE : 2 * TILE], scores[2 * TILE :]
                if has_rim:
                    oldest = oldest + bias
                    if tile == 0:
                        middle = middle + bias
                edge = jnp.where(causal, newest, oldest)
                peak = jnp.max(jnp.maximum(edge, middle), axis=0, keepdims=True)
                edge = jnp.exp2((edge - peak) * scale)
                middle = jnp.exp2((middle - peak) * scale)
                total = jnp.sum(edge + middle, axis=0, keepdims=True)
                edge = edge.astype(BF16)
                newest = edge * lower
                probs = jnp.concatenate([edge - newest, middle.astype(BF16), newest], axis=0)
                raw = dot(values_t[:, span], probs)
                mean = jnp.sum(raw * raw, axis=0, keepdims=True) * (1.0 / DH)
                scaled = raw * lax.rsqrt(mean + EPSILON * total * total) * gains[h]
                out_ref[block, head_columns(h), tile * TILE : (tile + 1) * TILE] = scaled.astype(BF16)


def attend_block(block, flags_ref, table_ref, index_ref, q_ref, near_ref, win_ref, gain_ref, bucket_refs):
    levels = len(bucket_refs)
    width = q_ref.shape[1]
    first = index_ref.shape[0] - levels
    tokens = pl.ds(pl.multiple_of(block * NEAR, NEAR), NEAR)
    index = index_ref[first:, tokens]
    attended = []
    for h in range(width // DH):
        at = head_columns(h)
        weights = weight_rows(index, table_ref, h, first)
        queries_t = q_ref[tokens, at].T
        lhs, rhs = [], []
        for level in range(levels):
            row = (weights[level : level + 1] * flags_ref[2, level]).astype(BF16)
            lhs.append(bucket_refs[level][at, :])
            rhs.append(queries_t * row)
        total = near_ref[block, at, :] + dot(jnp.concatenate(lhs, axis=1), jnp.concatenate(rhs, axis=0))
        mean = jnp.sum(total * total, axis=0, keepdims=True) * (1.0 / DH)
        gain = gain_column(gain_ref, h)
        gain = jnp.concatenate([gain] * (NEAR // DH), axis=1)
        total = total * lax.rsqrt(mean + EPSILON) * gain
        attended.append((total + win_ref[block, at, :].astype(F32)).astype(BF16).T)
    return jnp.concatenate(attended, axis=1)


def project(attended, w_ref, added, out_ref):
    step = 2 * DH
    for c in range(0, w_ref.shape[1], step):
        product = dot(attended, w_ref[:, c : c + step])
        for part in added:
            product = product + part[:, c : c + step].astype(F32)
        out_ref[:, c : c + step] = product.astype(BF16)


def first_block(away, head_count, pieces):
    return lax.rem(lax.axis_index("head") + away, head_count) * pieces


def partial_kernel(*refs, levels, away, head_count, pieces, piece):
    block = first_block(away, head_count, pieces) + piece
    project(attend_block(block, *refs[:7], refs[7 : 7 + levels]), refs[7 + levels], [], refs[-1])


def attend_kernel(*refs, levels, head_count, pieces):
    block = first_block(0, head_count, pieces) + pl.program_id(0)
    rows = pl.ds(pl.multiple_of(pl.program_id(0) * NEAR, NEAR), NEAR)
    refs[-1][rows, :] = attend_block(block, *refs[:7], refs[7 : 7 + levels])


def project_kernel(attended_ref, w_ref, *refs):
    added, out_ref = refs[:-1], refs[-1]
    pieces = len(added) * NEAR // out_ref.shape[0]
    for piece in range(out_ref.shape[0] // NEAR):
        rows = slice(piece * NEAR, (piece + 1) * NEAR)
        product = dot(attended_ref[rows, :], w_ref[...])
        for part in added[piece::out_ref.shape[0] // NEAR]:
            product = product + part[...].astype(F32)
        out_ref[rows, :] = product.astype(BF16)


def in_hbm(array):
    return pltpu.with_memory_space_constraint(array, pltpu.HBM)


SMEM = pl.BlockSpec(memory_space=pltpu.SMEM)
VMEM = pl.BlockSpec(memory_space=pltpu.VMEM)
HELD = pl.BlockSpec(memory_space=pl.ANY)


def make_shards(seq_count, head_count):
    def shards(
        queries,
        lin_keys,
        lin_values,
        window_keys,
        window_values,
        level_index,
        level_table,
        seq_lengths,
        gain_linear,
        gain_window,
        w_out,
    ):
        tokens, width_in = queries.shape
        heads = level_table.shape[1]
        groups = window_keys.shape[1] // DH
        members = heads // groups
        levels = seq_count.bit_length() - 1
        blocks = tokens // NEAR
        buckets = len(local_buckets(tokens))

        def params(megabytes):
            return pltpu.CompilerParams(vmem_limit_bytes=megabytes * MEGABYTE)

        keys, values, local_states, state, flags = pl.pallas_call(
            functools.partial(state_kernel, levels=levels),
            in_specs=[SMEM, HELD, HELD],
            out_specs=[VMEM, VMEM, VMEM, VMEM, SMEM],
            out_shape=[
                jax.ShapeDtypeStruct(lin_keys.shape, BF16),
                jax.ShapeDtypeStruct(lin_values.shape, BF16),
                jax.ShapeDtypeStruct((buckets, width_in, DH), BF16),
                jax.ShapeDtypeStruct((width_in, DH), BF16),
                jax.ShapeDtypeStruct((3, levels + 1), F32),
            ],
            scratch_shapes=[
                pltpu.VMEM((blocks, width_in, DH), F32),
                pltpu.SemaphoreType.DMA((2, blocks)),
            ],
            compiler_params=params(16),
            name="states",
        )(seq_lengths, in_hbm(lin_keys), in_hbm(lin_values))

        rim = jnp.concatenate([window_keys[tokens - WINDOW :], window_values[tokens - WINDOW :]], axis=1)

        def exchanged(level, state):
            return lax.ppermute(state, "seq", [(i, i ^ (1 << level)) for i in range(seq_count)])

        def joined(level, state, arrived, cover):
            return pl.pallas_call(
                functools.partial(join_kernel, level=level),
                in_specs=[SMEM, VMEM, VMEM] + [HELD] * len(cover),
                out_specs=VMEM,
                out_shape=jax.ShapeDtypeStruct(state.shape, BF16),
                compiler_params=params(4),
                name="join",
            )(flags, state, arrived, *cover)

        def neared(start, count, base):
            operands = [level_table, level_index, queries, keys, values, local_states]
            specs = [SMEM] + [VMEM] * 5
            aliases = {}
            if base is not None:
                aliases = {len(operands): 0}
                operands.append(base)
                specs.append(VMEM)
            return pl.pallas_call(
                functools.partial(near_kernel, spans=local_spans(tokens), start=start),
                grid=(count,),
                in_specs=specs,
                out_specs=VMEM,
                out_shape=jax.ShapeDtypeStruct((blocks, width_in, NEAR), F32),
                input_output_aliases=aliases,
                compiler_params=params(8),
                name="near",
            )(*operands)

        window_gains = gain_window.reshape(heads, 1, DH)

        def windowed(start, count, rim, base):
            operands = [flags, queries, window_keys, window_values, window_gains]
            specs = [SMEM] + [VMEM] * 4
            aliases = {}
            if rim is not None:
                operands.append(rim)
                specs.append(VMEM)
            if base is not None:
                aliases = {len(operands): 0}
                operands.append(base)
                specs.append(VMEM)
            return pl.pallas_call(
                functools.partial(window_kernel, has_rim=rim is not None, members=members, start=start),
                grid=(count,),
                in_specs=specs,
                out_specs=VMEM,
                scratch_shapes=[pltpu.VMEM((heads, DH, DH), F32)],
                out_shape=jax.ShapeDtypeStruct((blocks, width_in, NEAR), BF16),
                input_output_aliases=aliases,
                compiler_params=params(8),
                name="window",
            )(*operands)

        received = [exchanged(0, state)]
        near = neared(0, blocks, None)
        state = joined(0, state, received[0], [near])
        received.append(exchanged(1, state))
        windows = windowed(1, blocks - 1, None, None)
        cover = [windows]
        for level in range(1, levels - 1):
            state = joined(level, state, received[level], cover)
            received.append(exchanged(level + 1, state))
            cover = []
        rim = lax.ppermute(rim, "seq", [(i, (i + 1) % seq_count) for i in range(seq_count)])
        windows = windowed(0, 1, rim, windows)

        pieces = tokens // head_count // NEAR
        width = w_out.shape[1]
        shared = [flags, level_table, level_index, queries, near, windows]
        shared += [gain_linear.reshape(heads, 1, DH)] + received
        specs = [SMEM, SMEM] + [VMEM] * (5 + levels)

        arrived = []
        for away in range(1, head_count):
            route = [(i, (i + away) % head_count) for i in range(head_count)]
            for piece in range(pieces):
                partial = pl.pallas_call(
                    functools.partial(
                        partial_kernel,
                        levels=levels,
                        away=away,
                        head_count=head_count,
                        pieces=pieces,
                        piece=piece,
                    ),
                    in_specs=specs + [VMEM],
                    out_specs=VMEM,
                    out_shape=jax.ShapeDtypeStruct((NEAR, width), BF16),
                    compiler_params=params(8),
                    name="partial",
                )(*shared, w_out)
                arrived.append(lax.ppermute(partial, "head", route))
        attended = pl.pallas_call(
            functools.partial(attend_kernel, levels=levels, head_count=head_count, pieces=pieces),
            grid=(pieces,),
            in_specs=specs,
            out_specs=VMEM,
            out_shape=jax.ShapeDtypeStruct((pieces * NEAR, width_in), BF16),
            compiler_params=params(8),
            name="attend",
        )(*shared)
        step = 512
        return pl.pallas_call(
            project_kernel,
            grid=(width // step,),
            in_specs=[pl.BlockSpec((pieces * NEAR, width_in), lambda c: (0, 0))]
            + [pl.BlockSpec((width_in, step), lambda c: (0, c))]
            + [pl.BlockSpec((NEAR, step), lambda c: (0, c))] * len(arrived),
            out_specs=pl.BlockSpec((pieces * NEAR, step), lambda c: (0, c)),
            out_shape=jax.ShapeDtypeStruct((pieces * NEAR, width), BF16),
            compiler_params=params(12),
            name="project",
        )(attended, w_out, *arrived)

    return shards


def solution(mesh):
    placed = (
        P("seq", "head"),
        P("seq", "head"),
        P("seq", "head"),
        P("seq", "head"),
        P("seq", "head"),
        P(None, "seq"),
        P(None, "head"),
        P(),
        P("head"),
        P("head"),
        P("head", None),
    )
    return jax.shard_map(
        make_shards(mesh.shape["seq"], mesh.shape["head"]),
        mesh=mesh,
        in_specs=placed,
        out_specs=P(("seq", "head"), None),
        check_vma=False,
    )
```

```python
import functools

import jax
import jax.numpy as jnp
from jax import lax
from jax.experimental import pallas as pl
from jax.experimental.pallas import tpu as pltpu
from jax.sharding import PartitionSpec as P

DH = 128
WINDOW = 256
NEAR = 256
TILE = 128
GROUP = 8
EPSILON = 1e-06
LOG2_E = 1.4426950408889634
MEGABYTE = 1 << 20
BF16 = jnp.bfloat16
F32 = jnp.float32


def dot(a, b):
    return lax.dot_general(a, b, (((1,), (0,)), ((), ())), preferred_element_type=F32)


def dot_nt(a, b):
    return lax.dot_general(a, b, (((1,), (1,)), ((), ())), preferred_element_type=F32)


def local_spans(tokens):
    spans = []
    span = 1
    while span < tokens // NEAR:
        spans.append(span)
        span *= 2
    return spans


def local_buckets(tokens):
    blocks = tokens // NEAR
    return [(span, group) for span in local_spans(tokens) for group in range(1, blocks // span, 2)]


def weight_rows(index, table_ref, head, first_level):
    rows = jnp.zeros(index.shape, F32)
    for k in range(table_ref.shape[0]):
        rows = jnp.where(index == k, table_ref[k, head], rows)
    level = lax.broadcasted_iota(jnp.int32, index.shape, 0) + first_level
    return rows * jnp.exp2(-0.5 * level.astype(F32))


def head_columns(h):
    return slice(h * DH, (h + 1) * DH)


def state_kernel(
    lengths_hbm,
    k_hbm,
    v_hbm,
    wk_hbm,
    wv_hbm,
    k_ref,
    v_ref,
    rim_ref,
    local_ref,
    total_ref,
    flags_ref,
    states,
    lengths_ref,
    sems,
    rim_sems,
    lengths_sem,
    *,
    levels,
):
    blocks = states.shape[0]
    heads = k_ref.shape[1] // DH
    copies = []
    for b in range(blocks):
        rows = pl.ds(b * NEAR, NEAR)
        pair = [
            pltpu.make_async_copy(k_hbm.at[rows], k_ref.at[rows], sems.at[0, b]),
            pltpu.make_async_copy(v_hbm.at[rows], v_ref.at[rows], sems.at[1, b]),
        ]
        for copy in pair:
            copy.start()
        copies.append(pair)
    last_rows = pl.ds(wk_hbm.shape[0] - WINDOW, WINDOW)
    width = wk_hbm.shape[1]
    late = [
        pltpu.make_async_copy(wk_hbm.at[last_rows], rim_ref.at[:, pl.ds(0, width)], rim_sems.at[0]),
        pltpu.make_async_copy(wv_hbm.at[last_rows], rim_ref.at[:, pl.ds(width, width)], rim_sems.at[1]),
        pltpu.make_async_copy(lengths_hbm, lengths_ref, lengths_sem),
    ]
    for copy in late:
        copy.start()
    for b in range(blocks):
        rows = slice(b * NEAR, (b + 1) * NEAR)
        for copy in copies[b]:
            copy.wait()
        for h in range(heads):
            at = head_columns(h)
            states[b, at, :] = dot(v_ref[rows, at].T, k_ref[rows, at])
    for place, (span, group) in enumerate(local_buckets(blocks * NEAR)):
        members = [states[b] for b in range((group - 1) * span, group * span)]
        local_ref[place] = functools.reduce(jnp.add, members).astype(BF16)
    total_ref[...] = functools.reduce(jnp.add, [states[b] for b in range(blocks)]).astype(BF16)

    for copy in late:
        copy.wait()
    shard = lax.axis_index("seq")
    starts = [jnp.int32(0)]
    for s in range(lengths_ref.shape[0] - 1):
        starts.append(starts[-1] + lengths_ref[s])

    def begin_of(index):
        begin = jnp.int32(0)
        for start in starts[1:]:
            begin = jnp.where(start <= index, start, begin)
        return begin

    begin = begin_of(shard)
    rows = []
    for level in range(levels):
        last = shard | ((2 << level) - 1)
        middle = last - (1 << level)
        joined = jnp.where(begin_of(last) <= middle, 1.0, 0.0)
        right = (shard & (1 << level)) != 0
        rows.append(jnp.where(right, 1.0, joined))
        rows.append(jnp.where(right, joined, 1.0))
        rows.append(jnp.where(right & (begin <= middle), 1.0, 0.0))
    rows.append(jnp.where(begin == shard, -1e30, 0.0))
    for i, value in enumerate(rows):
        flags_ref[i : i + 1, :] = jnp.full((1, flags_ref.shape[1]), value, F32)


def flag_row(flags_ref, level, kind):
    return flags_ref[3 * level + kind : 3 * level + kind + 1, :]


def join_kernel(flags_ref, own_ref, arrived_ref, *rest, level):
    columns = own_ref.shape[1]
    own = own_ref[...] * flag_row(flags_ref, level, 0)[:, :columns].astype(BF16)
    rest[-1][...] = own + arrived_ref[...] * flag_row(flags_ref, level, 1)[:, :columns].astype(BF16)


def tile_mixing(weights):
    shape = (GROUP, TILE)
    row = lax.broadcasted_iota(jnp.int32, shape, 0)
    lane = lax.broadcasted_iota(jnp.int32, shape, 1)
    inner_bits = GROUP.bit_length() - 1
    within = lane % GROUP
    differ = row ^ within
    inner = jnp.where(differ == 0, weights[0:1], 0.0)
    for bit in range(inner_bits):
        inner = jnp.where((differ >> bit == 1) & (row < within), weights[bit + 1 : bit + 2], inner)
    shape = (TILE // GROUP, TILE)
    row = lax.broadcasted_iota(jnp.int32, shape, 0)
    above = lax.broadcasted_iota(jnp.int32, shape, 1) // GROUP
    differ = row ^ above
    outer = jnp.zeros(shape, F32)
    for bit in range((TILE // GROUP).bit_length() - 1):
        level = inner_bits + 1 + bit
        outer = jnp.where((differ >> bit == 1) & (row < above), weights[level : level + 1], outer)
    pieces = [
        jnp.where(lane // GROUP == g, inner, jnp.broadcast_to(outer[g : g + 1], (GROUP, TILE)))
        for g in range(TILE // GROUP)
    ]
    return jnp.concatenate(pieces, axis=0)


def near_kernel(table_ref, index_ref, q_ref, k_ref, v_ref, local_ref, *rest, spans, start):
    out_ref, weights_ref = rest[-2:]
    block = start + pl.program_id(0)
    blocks, width, _ = out_ref.shape
    near_bits = NEAR.bit_length() - 1
    tokens = pl.ds(pl.multiple_of(block * NEAR, NEAR), NEAR)
    index = index_ref[:, tokens]
    places, present = [], []
    first = 0
    for span in spans:
        group = block // span
        places.append(first + group // 2)
        present.append((group % 2).astype(F32))
        first += blocks // span // 2
    for h in range(width // DH):
        at = head_columns(h)
        weights = weight_rows(index, table_ref, h, 0)
        weights_ref[block, h] = weights
        queries_t = q_ref[tokens, at].T
        scores = dot(k_ref[tokens, at], queries_t)
        low = scores[:TILE, :TILE] * tile_mixing(weights[:, :TILE])
        cross = scores[:TILE, TILE:] * weights[near_bits : near_bits + 1, TILE:]
        high = scores[TILE:, TILE:] * tile_mixing(weights[:, TILE:])
        lhs = [v_ref[tokens, at].T]
        rhs = [
            jnp.concatenate([low.astype(BF16), cross.astype(BF16)], axis=1),
            jnp.concatenate([jnp.zeros((TILE, TILE), BF16), high.astype(BF16)], axis=1),
        ]
        for i, place in enumerate(places):
            level = near_bits + 1 + i
            row = (weights[level : level + 1] * present[i]).astype(BF16)
            lhs.append(local_ref[place, at, :])
            rhs.append(queries_t * row)
        out_ref[block, at, :] = dot(jnp.concatenate(lhs, axis=1), jnp.concatenate(rhs, axis=0))


def gain_column(gain_ref, h):
    return jnp.broadcast_to(gain_ref[h], (DH, DH)).T


def crosses_late(shard, seq_count):
    quarter = seq_count // 4
    return (shard % quarter == 0) & (shard != 2 * quarter)


def window_kernel(flags_ref, q_ref, k_ref, v_ref, gain_ref, *rest, has_rim, members, start):
    out_ref, gains = rest[-2:]
    block = start + pl.program_id(0)
    heads = q_ref.shape[1] // DH
    scale = LOG2_E * DH**-0.5

    @pl.when(pl.program_id(0) == 0)
    def _():
        for h in range(heads):
            gains[h] = gain_column(gain_ref, h)

    key_row = lax.broadcasted_iota(jnp.int32, (TILE, TILE), 0)
    query_lane = lax.broadcasted_iota(jnp.int32, (TILE, TILE), 1)
    causal = key_row <= query_lane
    lower = jnp.where(causal, 1.0, 0.0).astype(BF16)
    now = pl.multiple_of(block * NEAR, NEAR)
    if has_rim:
        bias = flags_ref[flags_ref.shape[0] - 1 :, :TILE]
    for g in range(heads // members):
        at = head_columns(g)
        if has_rim:
            is_late = crosses_late(lax.axis_index("seq"), lax.axis_size("seq"))
            beside = head_columns(g + heads // members)
            old_k = jnp.where(is_late, rest[1][:, at], rest[0][:, at])
            old_v = jnp.where(is_late, rest[1][:, beside], rest[0][:, beside])
        else:
            old_k = k_ref[pl.ds(now - WINDOW, WINDOW), at]
            old_v = v_ref[pl.ds(now - WINDOW, WINDOW), at]
        keys = jnp.concatenate([old_k, k_ref[pl.ds(now, NEAR), at]], axis=0)
        values_t = jnp.concatenate([old_v.T, v_ref[pl.ds(now, NEAR), at].T], axis=1)
        for h in range(g * members, (g + 1) * members):
            for tile in range(NEAR // TILE):
                queries = q_ref[pl.ds(now + tile * TILE, TILE), head_columns(h)]
                span = slice(tile * TILE, tile * TILE + WINDOW + TILE)
                scores = dot_nt(keys[span], queries)
                oldest, middle, newest = scores[:TILE], scores[TILE : 2 * TILE], scores[2 * TILE :]
                if has_rim:
                    oldest = oldest + bias
                    if tile == 0:
                        middle = middle + bias
                edge = jnp.where(causal, newest, oldest)
                peak = jnp.max(jnp.maximum(edge, middle), axis=0, keepdims=True)
                edge = jnp.exp2((edge - peak) * scale)
                middle = jnp.exp2((middle - peak) * scale)
                total = jnp.sum(edge + middle, axis=0, keepdims=True)
                edge = edge.astype(BF16)
                newest = edge * lower
                probs = jnp.concatenate([edge - newest, middle.astype(BF16), newest], axis=0)
                raw = dot(values_t[:, span], probs)
                mean = jnp.sum(raw * raw, axis=0, keepdims=True) * (1.0 / DH)
                scaled = raw * lax.rsqrt(mean + EPSILON * total * total) * gains[h]
                out_ref[block, head_columns(h), tile * TILE : (tile + 1) * TILE] = scaled.astype(BF16)


def far_terms(block, first, h, flags_ref, weights_ref, q_ref, bucket_refs):
    above = weights_ref.shape[2] - flags_ref.shape[0] // 3 + first
    tokens = pl.ds(pl.multiple_of(block * NEAR, NEAR), NEAR)
    at = head_columns(h)
    queries_t = q_ref[tokens, at].T
    lhs, rhs = [], []
    for i, bucket_ref in enumerate(bucket_refs):
        row = weights_ref[block, h, above + i : above + i + 1, :] * flag_row(flags_ref, first + i, 2)
        lhs.append(bucket_ref[at, :])
        rhs.append(queries_t * row.astype(BF16))
    return dot(jnp.concatenate(lhs, axis=1), jnp.concatenate(rhs, axis=0))


def far_kernel(flags_ref, weights_ref, q_ref, near_ref, *rest):
    bucket_refs, out_ref = rest[:-1], rest[-1]
    block = pl.program_id(0)
    for h in range(q_ref.shape[1] // DH):
        at = head_columns(h)
        reached = far_terms(block, 0, h, flags_ref, weights_ref, q_ref, bucket_refs)
        out_ref[block, at, :] = near_ref[block, at, :] + reached


def attend_block(block, flags_ref, weights_ref, q_ref, near_ref, win_ref, gain_ref, bucket_ref):
    last = flags_ref.shape[0] // 3 - 1
    attended = []
    for h in range(q_ref.shape[1] // DH):
        at = head_columns(h)
        reached = far_terms(block, last, h, flags_ref, weights_ref, q_ref, [bucket_ref])
        total = near_ref[block, at, :] + reached
        mean = jnp.sum(total * total, axis=0, keepdims=True) * (1.0 / DH)
        gain = gain_column(gain_ref, h)
        gain = jnp.concatenate([gain] * (NEAR // DH), axis=1)
        total = total * lax.rsqrt(mean + EPSILON) * gain
        attended.append((total + win_ref[block, at, :].astype(F32)).astype(BF16).T)
    return jnp.concatenate(attended, axis=1)


def project(attended, w_ref, added, out_ref):
    step = 2 * DH
    for c in range(0, w_ref.shape[1], step):
        product = dot(attended, w_ref[:, c : c + step])
        for part in added:
            product = product + part[:, c : c + step].astype(F32)
        out_ref[:, c : c + step] = product.astype(BF16)


def first_block(away, head_count, pieces):
    return lax.rem(lax.axis_index("head") + away, head_count) * pieces


def partial_kernel(*refs, away, head_count, pieces, piece):
    block = first_block(away, head_count, pieces) + piece
    project(attend_block(block, *refs[:7]), refs[7], [], refs[-1])


def attend_kernel(*refs, head_count, pieces, piece):
    block = first_block(0, head_count, pieces) + piece
    refs[-1][...] = attend_block(block, *refs[:7])


def project_kernel(attended_ref, w_ref, *refs):
    project(attended_ref[...], w_ref, refs[:-1], refs[-1])


def last_kernel(*refs, head_count, pieces, others):
    w_ref = refs[7]
    added = refs[8 : 8 + others]
    done = refs[8 + others : 8 + others + pieces - 1]
    out_ref, result, sems = refs[8 + others + pieces - 1 :]
    copies = []
    for piece, source in enumerate(done):
        rows = pl.ds(piece * NEAR, NEAR)
        copies.append(pltpu.make_async_copy(source, out_ref.at[rows], sems.at[piece]))
        copies[-1].start()
    attended = attend_block(first_block(0, head_count, pieces) + pieces - 1, *refs[:7])
    step = w_ref.shape[1] // (sems.shape[0] - pieces + 1)
    rows = pl.ds((pieces - 1) * NEAR, NEAR)
    for i, c in enumerate(range(0, w_ref.shape[1], step)):
        columns = slice(c, c + step)
        product = dot(attended, w_ref[:, columns])
        for part in added:
            product = product + part[:, columns].astype(F32)
        result[:, columns] = product.astype(BF16)
        at = pl.ds(c, step)
        copy = pltpu.make_async_copy(result.at[:, at], out_ref.at[rows, at], sems.at[pieces - 1 + i])
        copy.start()
        copies.append(copy)
    for copy in copies:
        copy.wait()


def in_hbm(array):
    return pltpu.with_memory_space_constraint(array, pltpu.HBM)


SMEM = pl.BlockSpec(memory_space=pltpu.SMEM)
VMEM = pl.BlockSpec(memory_space=pltpu.VMEM)
HELD = pl.BlockSpec(memory_space=pl.ANY)


def make_shards(seq_count, head_count):
    def layer(
        queries,
        lin_keys,
        lin_values,
        window_keys,
        window_values,
        level_index,
        level_table,
        seq_lengths,
        gain_linear,
        gain_window,
        w_out,
    ):
        tokens, width_in = queries.shape
        heads = level_table.shape[1]
        groups = window_keys.shape[1] // DH
        members = heads // groups
        levels = seq_count.bit_length() - 1
        blocks = tokens // NEAR
        buckets = len(local_buckets(tokens))

        def params(megabytes):
            return pltpu.CompilerParams(vmem_limit_bytes=megabytes * MEGABYTE)

        states_call = pl.pallas_call(
            functools.partial(state_kernel, levels=levels),
            in_specs=[HELD] * 5,
            out_specs=[VMEM] * 6,
            out_shape=[
                jax.ShapeDtypeStruct(lin_keys.shape, BF16),
                jax.ShapeDtypeStruct(lin_values.shape, BF16),
                jax.ShapeDtypeStruct((WINDOW, 2 * window_keys.shape[1]), BF16),
                jax.ShapeDtypeStruct((buckets, width_in, DH), BF16),
                jax.ShapeDtypeStruct((width_in, DH), BF16),
                jax.ShapeDtypeStruct((3 * levels + 1, NEAR), F32),
            ],
            scratch_shapes=[
                pltpu.VMEM((blocks, width_in, DH), F32),
                pltpu.SMEM(seq_lengths.shape, jnp.int32),
                pltpu.SemaphoreType.DMA((2, blocks)),
                pltpu.SemaphoreType.DMA((2,)),
                pltpu.SemaphoreType.DMA,
            ],
            compiler_params=params(16),
            name="states",
        )
        keys, values, rim, local_states, state, flags = states_call(
            *[in_hbm(a) for a in (seq_lengths, lin_keys, lin_values, window_keys, window_values)]
        )

        def exchanged(level, state):
            route = [(i, i ^ (1 << level)) for i in range(seq_count)]
            return lax.ppermute(state, "seq", route)

        def joined(level, state, arrived, cover):
            return pl.pallas_call(
                functools.partial(join_kernel, level=level),
                in_specs=[VMEM, VMEM, VMEM] + [HELD] * len(cover),
                out_specs=VMEM,
                out_shape=jax.ShapeDtypeStruct(state.shape, BF16),
                compiler_params=params(4),
                name="join",
            )(flags, state, arrived, *cover)

        def neared(start, count, base):
            operands = [level_table, level_index, queries, keys, values, local_states]
            specs = [SMEM] + [VMEM] * 5
            aliases = {}
            if base is not None:
                aliases = {len(operands): 0}
                operands.append(base)
                specs.append(VMEM)
            return pl.pallas_call(
                functools.partial(near_kernel, spans=local_spans(tokens), start=start),
                grid=(count,),
                in_specs=specs,
                out_specs=[VMEM, VMEM],
                out_shape=[
                    jax.ShapeDtypeStruct((blocks, width_in, NEAR), F32),
                    jax.ShapeDtypeStruct((blocks, heads, level_index.shape[0], NEAR), F32),
                ],
                input_output_aliases=aliases,
                compiler_params=params(8),
                name="near",
            )(*operands)

        window_gains = gain_window.reshape(heads, 1, DH)

        def windowed(start, count, rim, base):
            operands = [flags, queries, window_keys, window_values, window_gains]
            specs = [VMEM] * 5
            aliases = {}
            if rim is not None:
                operands += rim
                specs += [VMEM] * len(rim)
            if base is not None:
                aliases = {len(operands): 0}
                operands.append(base)
                specs.append(VMEM)
            return pl.pallas_call(
                functools.partial(window_kernel, has_rim=rim is not None, members=members, start=start),
                grid=(count,),
                in_specs=specs,
                out_specs=VMEM,
                scratch_shapes=[pltpu.VMEM((heads, DH, DH), F32)],
                out_shape=jax.ShapeDtypeStruct((blocks, width_in, NEAR), BF16),
                input_output_aliases=aliases,
                compiler_params=params(8),
                name="window",
            )(*operands)

        received = [exchanged(0, state)]
        near, weights = neared(0, blocks, None)
        state = joined(0, state, received[0], [near])
        received.append(exchanged(1, state))
        windows = windowed(1, blocks - 1, None, None)
        cover = [windows]
        steps = [(i, i + 1) for i in range(seq_count - 1)]
        late = [(i, j) for i, j in steps if crosses_late(j, seq_count)]
        for level in range(1, levels - 1):
            if level == levels - 2:
                early_rim = lax.ppermute(rim, "seq", [step for step in steps if step not in late])
            state = joined(level, state, received[level], cover)
            received.append(exchanged(level + 1, state))
            cover = []
        late_rim = lax.ppermute(rim, "seq", late)
        windows = windowed(0, 1, (early_rim, late_rim), windows)
        near = pl.pallas_call(
            far_kernel,
            grid=(blocks,),
            in_specs=[VMEM] * (3 + levels),
            out_specs=VMEM,
            out_shape=jax.ShapeDtypeStruct(near.shape, F32),
            input_output_aliases={3: 0},
            compiler_params=params(8),
            name="far",
        )(flags, weights, queries, near, *received[:-1])

        pieces = tokens // head_count // NEAR
        width = w_out.shape[1]
        shared = [flags, weights, queries, near, windows]
        shared += [gain_linear.reshape(heads, 1, DH), received[-1]]
        specs = [VMEM] * 7

        arrived = [[] for _ in range(pieces)]
        for away in range(1, head_count):
            route = [(i, (i + away) % head_count) for i in range(head_count)]
            for piece in range(pieces):
                partial = pl.pallas_call(
                    functools.partial(
                        partial_kernel, away=away, head_count=head_count, pieces=pieces, piece=piece
                    ),
                    in_specs=specs + [VMEM],
                    out_specs=VMEM,
                    out_shape=jax.ShapeDtypeStruct((NEAR, width), BF16),
                    compiler_params=params(8),
                    name="partial",
                )(*shared, w_out)
                arrived[piece].append(lax.ppermute(partial, "head", route))
        finished = []
        for piece in range(pieces - 1):
            attended = pl.pallas_call(
                functools.partial(attend_kernel, head_count=head_count, pieces=pieces, piece=piece),
                in_specs=specs,
                out_specs=VMEM,
                out_shape=jax.ShapeDtypeStruct((NEAR, width_in), BF16),
                compiler_params=params(8),
                name="attend",
            )(*shared)
            finished.append(
                pl.pallas_call(
                    project_kernel,
                    in_specs=[VMEM] * (2 + len(arrived[piece])),
                    out_specs=VMEM,
                    out_shape=jax.ShapeDtypeStruct((NEAR, width), BF16),
                    compiler_params=params(8),
                    name="project",
                )(attended, w_out, *arrived[piece])
            )
        others = len(arrived[-1])
        parts = 4
        return pl.pallas_call(
            functools.partial(last_kernel, head_count=head_count, pieces=pieces, others=others),
            in_specs=specs + [VMEM] * (others + pieces),
            out_specs=HELD,
            out_shape=jax.ShapeDtypeStruct((pieces * NEAR, width), BF16),
            scratch_shapes=[
                pltpu.VMEM((NEAR, width), BF16),
                pltpu.SemaphoreType.DMA((pieces - 1 + parts,)),
            ],
            compiler_params=params(8),
            name="last",
        )(*shared, w_out, *arrived[-1], *finished)

    return layer


def solution(mesh):
    placed = (
        P("seq", "head"),
        P("seq", "head"),
        P("seq", "head"),
        P("seq", "head"),
        P("seq", "head"),
        P(None, "seq"),
        P(None, "head"),
        P(),
        P("head"),
        P("head"),
        P("head", None),
    )
    return jax.shard_map(
        make_shards(mesh.shape["seq"], mesh.shape["head"]),
        mesh=mesh,
        in_specs=placed,
        out_specs=P(("seq", "head"), None),
        check_vma=False,
    )
```

```python
import functools

import jax
import jax.numpy as jnp
from jax import lax
from jax.experimental import pallas as pl
from jax.experimental.pallas import tpu as pltpu
from jax.sharding import PartitionSpec as P

DH = 128
WINDOW = 256
NEAR = 256
TILE = 128
GROUP = 8
EPSILON = 1e-06
LOG2_E = 1.4426950408889634
MEGABYTE = 1 << 20
BF16 = jnp.bfloat16
F32 = jnp.float32


def dot(a, b):
    return lax.dot_general(a, b, (((1,), (0,)), ((), ())), preferred_element_type=F32)


def dot_nt(a, b):
    return lax.dot_general(a, b, (((1,), (1,)), ((), ())), preferred_element_type=F32)


def local_spans(tokens):
    spans = []
    span = 1
    while span < tokens // NEAR:
        spans.append(span)
        span *= 2
    return spans


def local_buckets(tokens):
    blocks = tokens // NEAR
    return [(span, group) for span in local_spans(tokens) for group in range(1, blocks // span, 2)]


def weight_rows(index, table_ref, head, first_level):
    rows = jnp.zeros(index.shape, F32)
    for k in range(table_ref.shape[0]):
        rows = jnp.where(index == k, table_ref[k, head], rows)
    level = lax.broadcasted_iota(jnp.int32, index.shape, 0) + first_level
    return rows * jnp.exp2(-0.5 * level.astype(F32))


def head_columns(h):
    return slice(h * DH, (h + 1) * DH)


def state_kernel(
    lengths_hbm,
    k_hbm,
    v_hbm,
    wk_hbm,
    wv_hbm,
    k_ref,
    v_ref,
    rim_ref,
    local_ref,
    total_a_ref,
    total_b_ref,
    flags_ref,
    states,
    lengths_ref,
    sems,
    rim_sems,
    lengths_sem,
    *,
    levels,
):
    blocks = states.shape[0]
    heads = k_ref.shape[1] // DH
    copies = []
    for b in range(blocks):
        rows = pl.ds(b * NEAR, NEAR)
        pair = [
            pltpu.make_async_copy(k_hbm.at[rows], k_ref.at[rows], sems.at[0, b]),
            pltpu.make_async_copy(v_hbm.at[rows], v_ref.at[rows], sems.at[1, b]),
        ]
        for copy in pair:
            copy.start()
        copies.append(pair)
    last_rows = pl.ds(wk_hbm.shape[0] - WINDOW, WINDOW)
    width = wk_hbm.shape[1]
    late = [
        pltpu.make_async_copy(wk_hbm.at[last_rows], rim_ref.at[:, pl.ds(0, width)], rim_sems.at[0]),
        pltpu.make_async_copy(wv_hbm.at[last_rows], rim_ref.at[:, pl.ds(width, width)], rim_sems.at[1]),
        pltpu.make_async_copy(lengths_hbm, lengths_ref, lengths_sem),
    ]
    for copy in late:
        copy.start()
    for b in range(blocks):
        rows = slice(b * NEAR, (b + 1) * NEAR)
        for copy in copies[b]:
            copy.wait()
        for h in range(heads):
            at = head_columns(h)
            states[b, at, :] = dot(v_ref[rows, at].T, k_ref[rows, at])
    for place, (span, group) in enumerate(local_buckets(blocks * NEAR)):
        members = [states[b] for b in range((group - 1) * span, group * span)]
        local_ref[place] = functools.reduce(jnp.add, members).astype(BF16)
    middle_row = total_a_ref.shape[0]
    for total_ref, rows in ((total_a_ref, slice(0, middle_row)), (total_b_ref, slice(middle_row, None))):
        members = [states[b, rows, :] for b in range(blocks)]
        total_ref[...] = functools.reduce(jnp.add, members).astype(BF16)

    for copy in late:
        copy.wait()
    shard = lax.axis_index("seq")
    starts = [jnp.int32(0)]
    for s in range(lengths_ref.shape[0] - 1):
        starts.append(starts[-1] + lengths_ref[s])

    def begin_of(index):
        begin = jnp.int32(0)
        for start in starts[1:]:
            begin = jnp.where(start <= index, start, begin)
        return begin

    begin = begin_of(shard)
    rows = []
    for level in range(levels):
        last = shard | ((2 << level) - 1)
        middle = last - (1 << level)
        joined = jnp.where(begin_of(last) <= middle, 1.0, 0.0)
        right = (shard & (1 << level)) != 0
        rows.append(jnp.where(right, 1.0, joined))
        rows.append(jnp.where(right, joined, 1.0))
        rows.append(jnp.where(right & (begin <= middle), 1.0, 0.0))
    rows.append(jnp.where(begin == shard, -1e30, 0.0))
    for i, value in enumerate(rows):
        flags_ref[i : i + 1, :] = jnp.full((1, flags_ref.shape[1]), value, F32)


def flag_row(flags_ref, level, kind):
    return flags_ref[3 * level + kind : 3 * level + kind + 1, :]


def join_kernel(flags_ref, own_ref, arrived_ref, *rest, level):
    columns = own_ref.shape[1]
    own = own_ref[...] * flag_row(flags_ref, level, 0)[:, :columns].astype(BF16)
    rest[-1][...] = own + arrived_ref[...] * flag_row(flags_ref, level, 1)[:, :columns].astype(BF16)


def tile_mixing(weights):
    shape = (GROUP, TILE)
    row = lax.broadcasted_iota(jnp.int32, shape, 0)
    lane = lax.broadcasted_iota(jnp.int32, shape, 1)
    inner_bits = GROUP.bit_length() - 1
    within = lane % GROUP
    differ = row ^ within
    inner = jnp.where(differ == 0, weights[0:1], 0.0)
    for bit in range(inner_bits):
        inner = jnp.where((differ >> bit == 1) & (row < within), weights[bit + 1 : bit + 2], inner)
    shape = (TILE // GROUP, TILE)
    row = lax.broadcasted_iota(jnp.int32, shape, 0)
    above = lax.broadcasted_iota(jnp.int32, shape, 1) // GROUP
    differ = row ^ above
    outer = jnp.zeros(shape, F32)
    for bit in range((TILE // GROUP).bit_length() - 1):
        level = inner_bits + 1 + bit
        outer = jnp.where((differ >> bit == 1) & (row < above), weights[level : level + 1], outer)
    pieces = [
        jnp.where(lane // GROUP == g, inner, jnp.broadcast_to(outer[g : g + 1], (GROUP, TILE)))
        for g in range(TILE // GROUP)
    ]
    return jnp.concatenate(pieces, axis=0)


def weights_kernel(table_ref, index_ref, weights_ref):
    for h in range(weights_ref.shape[0]):
        weights_ref[h] = weight_rows(index_ref[...], table_ref, h, 0)


def near_kernel(weights_ref, q_ref, k_ref, v_ref, local_ref, *rest, spans, start):
    out_ref, token_ref = rest[-2:]
    token_ref[...] = jnp.zeros(token_ref.shape, F32)
    block = start + pl.program_id(0)
    blocks, width, _ = out_ref.shape
    near_bits = NEAR.bit_length() - 1
    tokens = pl.ds(pl.multiple_of(block * NEAR, NEAR), NEAR)
    places, present = [], []
    first = 0
    for span in spans:
        group = block // span
        places.append(first + group // 2)
        present.append((group % 2).astype(F32))
        first += blocks // span // 2
    for h in range(width // DH):
        at = head_columns(h)
        weights = weights_ref[h, :, tokens]
        queries_t = q_ref[tokens, at].T
        scores = dot(k_ref[tokens, at], queries_t)
        low = scores[:TILE, :TILE] * tile_mixing(weights[:, :TILE])
        cross = scores[:TILE, TILE:] * weights[near_bits : near_bits + 1, TILE:]
        high = scores[TILE:, TILE:] * tile_mixing(weights[:, TILE:])
        lhs = [v_ref[tokens, at].T]
        rhs = [
            jnp.concatenate([low.astype(BF16), cross.astype(BF16)], axis=1),
            jnp.concatenate([jnp.zeros((TILE, TILE), BF16), high.astype(BF16)], axis=1),
        ]
        for i, place in enumerate(places):
            level = near_bits + 1 + i
            row = (weights[level : level + 1] * present[i]).astype(BF16)
            lhs.append(local_ref[place, at, :])
            rhs.append(queries_t * row)
        out_ref[block, at, :] = dot(jnp.concatenate(lhs, axis=1), jnp.concatenate(rhs, axis=0))


def gain_column(gain_ref, h):
    return jnp.broadcast_to(gain_ref[h], (DH, DH)).T


def pick_kernel(own_ref, ahead_ref, out_ref, *, plane):
    closes = lax.axis_index("seq") % plane == plane - 1
    out_ref[...] = jnp.where(closes, ahead_ref[...], own_ref[...])


def window_kernel(flags_ref, q_ref, k_ref, v_ref, gain_ref, *rest, has_rim, members, start):
    out_ref, token_ref, gains = rest[-3:]
    token_ref[...] = jnp.zeros(token_ref.shape, F32)
    block = start + pl.program_id(0)
    heads = q_ref.shape[1] // DH
    scale = LOG2_E * DH**-0.5

    @pl.when(pl.program_id(0) == 0)
    def _():
        for h in range(heads):
            gains[h] = gain_column(gain_ref, h)

    key_row = lax.broadcasted_iota(jnp.int32, (TILE, TILE), 0)
    query_lane = lax.broadcasted_iota(jnp.int32, (TILE, TILE), 1)
    causal = key_row <= query_lane
    lower = jnp.where(causal, 1.0, 0.0).astype(BF16)
    now = pl.multiple_of(block * NEAR, NEAR)
    if has_rim:
        bias = flags_ref[flags_ref.shape[0] - 1 :, :TILE]
    for g in range(heads // members):
        at = head_columns(g)
        if has_rim:
            old_k = rest[0][:, at]
            old_v = rest[0][:, head_columns(g + heads // members)]
        else:
            old_k = k_ref[pl.ds(now - WINDOW, WINDOW), at]
            old_v = v_ref[pl.ds(now - WINDOW, WINDOW), at]
        keys = jnp.concatenate([old_k, k_ref[pl.ds(now, NEAR), at]], axis=0)
        values_t = jnp.concatenate([old_v.T, v_ref[pl.ds(now, NEAR), at].T], axis=1)
        for h in range(g * members, (g + 1) * members):
            for tile in range(NEAR // TILE):
                queries = q_ref[pl.ds(now + tile * TILE, TILE), head_columns(h)]
                span = slice(tile * TILE, tile * TILE + WINDOW + TILE)
                scores = dot_nt(keys[span], queries)
                oldest, middle, newest = scores[:TILE], scores[TILE : 2 * TILE], scores[2 * TILE :]
                if has_rim:
                    oldest = oldest + bias
                    if tile == 0:
                        middle = middle + bias
                edge = jnp.where(causal, newest, oldest)
                peak = jnp.max(jnp.maximum(edge, middle), axis=0, keepdims=True)
                edge = jnp.exp2((edge - peak) * scale)
                middle = jnp.exp2((middle - peak) * scale)
                total = jnp.sum(edge + middle, axis=0, keepdims=True)
                edge = edge.astype(BF16)
                newest = edge * lower
                probs = jnp.concatenate([edge - newest, middle.astype(BF16), newest], axis=0)
                raw = dot(values_t[:, span], probs)
                mean = jnp.sum(raw * raw, axis=0, keepdims=True) * (1.0 / DH)
                scaled = raw * lax.rsqrt(mean + EPSILON * total * total) * gains[h]
                out_ref[block, head_columns(h), tile * TILE : (tile + 1) * TILE] = scaled.astype(BF16)


def far_terms(block, first, h, flags_ref, weights_ref, q_ref, bucket_refs):
    above = weights_ref.shape[1] - flags_ref.shape[0] // 3 + first
    tokens = pl.ds(pl.multiple_of(block * NEAR, NEAR), NEAR)
    queries_t = q_ref[tokens, head_columns(h)].T
    half = q_ref.shape[1] // 2 // DH
    lhs, rhs = [], []
    for i in range(len(bucket_refs) // 2):
        level = slice(above + i, above + i + 1)
        row = weights_ref[h, level, tokens] * flag_row(flags_ref, first + i, 2)
        lhs.append(bucket_refs[2 * i + h // half][head_columns(h % half), :])
        rhs.append(queries_t * row.astype(BF16))
    return dot(jnp.concatenate(lhs, axis=1), jnp.concatenate(rhs, axis=0))


def far_kernel(flags_ref, weights_ref, q_ref, near_ref, *rest):
    bucket_refs, out_ref = rest[:-1], rest[-1]
    block = pl.program_id(0)
    for h in range(q_ref.shape[1] // DH):
        at = head_columns(h)
        reached = far_terms(block, 0, h, flags_ref, weights_ref, q_ref, bucket_refs)
        out_ref[block, at, :] = near_ref[block, at, :] + reached


def attend_block(block, flags_ref, weights_ref, q_ref, near_ref, win_ref, gain_ref, *bucket_refs):
    last = flags_ref.shape[0] // 3 - 1
    attended = []
    for h in range(q_ref.shape[1] // DH):
        at = head_columns(h)
        reached = far_terms(block, last, h, flags_ref, weights_ref, q_ref, bucket_refs)
        total = near_ref[block, at, :] + reached
        mean = jnp.sum(total * total, axis=0, keepdims=True) * (1.0 / DH)
        gain = gain_column(gain_ref, h)
        gain = jnp.concatenate([gain] * (NEAR // DH), axis=1)
        total = total * lax.rsqrt(mean + EPSILON) * gain
        attended.append((total + win_ref[block, at, :].astype(F32)).astype(BF16).T)
    return jnp.concatenate(attended, axis=1)


def project(attended, w_ref, added, out_ref):
    step = 2 * DH
    for c in range(0, w_ref.shape[1], step):
        product = dot(attended, w_ref[:, c : c + step])
        for part in added:
            product = product + part[:, c : c + step].astype(F32)
        out_ref[:, c : c + step] = product.astype(BF16)


def first_block(away, head_count, pieces):
    return lax.rem(lax.axis_index("head") + away, head_count) * pieces


def partial_kernel(*refs, away, head_count, pieces, piece):
    block = first_block(away, head_count, pieces) + piece
    project(attend_block(block, *refs[:8]), refs[8], [], refs[-1])


def attend_kernel(*refs, head_count, pieces, piece):
    block = first_block(0, head_count, pieces) + piece
    refs[-1][...] = attend_block(block, *refs[:8])


def project_kernel(attended_ref, w_ref, *refs):
    project(attended_ref[...], w_ref, refs[:-1], refs[-1])


def last_kernel(*refs, head_count, pieces, others):
    w_ref = refs[8]
    added = refs[9 : 9 + others]
    done = refs[9 + others : 8 + others + pieces]
    out_ref, result, sems = refs[8 + others + pieces :]
    copies = []
    for piece, source in enumerate(done):
        rows = pl.ds(piece * NEAR, NEAR)
        copies.append(pltpu.make_async_copy(source, out_ref.at[rows], sems.at[piece]))
        copies[-1].start()
    attended = attend_block(first_block(0, head_count, pieces) + pieces - 1, *refs[:8])
    step = w_ref.shape[1] // (sems.shape[0] - pieces + 1)
    rows = pl.ds((pieces - 1) * NEAR, NEAR)
    for i, c in enumerate(range(0, w_ref.shape[1], step)):
        columns = slice(c, c + step)
        product = dot(attended, w_ref[:, columns])
        for part in added:
            product = product + part[:, columns].astype(F32)
        result[:, columns] = product.astype(BF16)
        at = pl.ds(c, step)
        copy = pltpu.make_async_copy(result.at[:, at], out_ref.at[rows, at], sems.at[pieces - 1 + i])
        copy.start()
        copies.append(copy)
    for copy in copies:
        copy.wait()


def in_hbm(array):
    return pltpu.with_memory_space_constraint(array, pltpu.HBM)


SMEM = pl.BlockSpec(memory_space=pltpu.SMEM)
VMEM = pl.BlockSpec(memory_space=pltpu.VMEM)
HELD = pl.BlockSpec(memory_space=pl.ANY)


COVERS = {
    ("a", 0): ("near", 0, 2),
    ("b", 0): ("near", 2, 1),
    ("a", 1): ("near", 3, 1),
    ("b", 1): ("window", 1, 1),
    ("a", 2): ("window", 2, 1),
    ("b", 2): ("window", 3, 1),
}


def make_shards(seq_count, head_count):
    def layer(
        queries,
        lin_keys,
        lin_values,
        window_keys,
        window_values,
        level_index,
        level_table,
        seq_lengths,
        gain_linear,
        gain_window,
        w_out,
    ):
        tokens, width_in = queries.shape
        heads = level_table.shape[1]
        groups = window_keys.shape[1] // DH
        members = heads // groups
        levels = seq_count.bit_length() - 1
        blocks = tokens // NEAR
        buckets = len(local_buckets(tokens))

        def params(megabytes):
            return pltpu.CompilerParams(vmem_limit_bytes=megabytes * MEGABYTE)

        states_call = pl.pallas_call(
            functools.partial(state_kernel, levels=levels),
            in_specs=[HELD] * 5,
            out_specs=[VMEM] * 7,
            out_shape=[
                jax.ShapeDtypeStruct(lin_keys.shape, BF16),
                jax.ShapeDtypeStruct(lin_values.shape, BF16),
                jax.ShapeDtypeStruct((WINDOW, 2 * window_keys.shape[1]), BF16),
                jax.ShapeDtypeStruct((buckets, width_in, DH), BF16),
                jax.ShapeDtypeStruct((width_in // 2, DH), BF16),
                jax.ShapeDtypeStruct((width_in // 2, DH), BF16),
                jax.ShapeDtypeStruct((3 * levels + 1, NEAR), F32),
            ],
            scratch_shapes=[
                pltpu.VMEM((blocks, width_in, DH), F32),
                pltpu.SMEM(seq_lengths.shape, jnp.int32),
                pltpu.SemaphoreType.DMA((2, blocks)),
                pltpu.SemaphoreType.DMA((2,)),
                pltpu.SemaphoreType.DMA,
            ],
            compiler_params=params(16),
            name="states",
        )
        keys, values, rim, local_states, state_a, state_b, flags = states_call(
            *[in_hbm(a) for a in (seq_lengths, lin_keys, lin_values, window_keys, window_values)]
        )

        def exchanged(level, state):
            route = [(i, i ^ (1 << level)) for i in range(seq_count)]
            return lax.ppermute(state, "seq", route)

        def joined(level, state, arrived, cover):
            return pl.pallas_call(
                functools.partial(join_kernel, level=level),
                in_specs=[VMEM] * (3 + len(cover)),
                out_specs=VMEM,
                out_shape=jax.ShapeDtypeStruct(state.shape, BF16),
                compiler_params=params(4),
                name="join",
            )(flags, state, arrived, *cover)

        token = jax.ShapeDtypeStruct((GROUP, TILE), F32)
        weights = pl.pallas_call(
            weights_kernel,
            in_specs=[SMEM, VMEM],
            out_specs=VMEM,
            out_shape=jax.ShapeDtypeStruct((heads, *level_index.shape), F32),
            compiler_params=params(8),
            name="weights",
        )(level_table, level_index)

        def neared(start, count, base):
            operands = [weights, queries, keys, values, local_states]
            aliases = {}
            if base is not None:
                aliases = {len(operands): 0}
                operands.append(base)
            return pl.pallas_call(
                functools.partial(near_kernel, spans=local_spans(tokens), start=start),
                grid=(count,),
                in_specs=[VMEM] * len(operands),
                out_specs=[VMEM, VMEM],
                out_shape=[jax.ShapeDtypeStruct((blocks, width_in, NEAR), F32), token],
                input_output_aliases=aliases,
                compiler_params=params(8),
                name="near",
            )(*operands)

        window_gains = gain_window.reshape(heads, 1, DH)

        def windowed(start, count, rim, base):
            operands = [flags, queries, window_keys, window_values, window_gains]
            aliases = {}
            if rim is not None:
                operands += rim
            if base is not None:
                aliases = {len(operands): 0}
                operands.append(base)
            return pl.pallas_call(
                functools.partial(
                    window_kernel, has_rim=rim is not None, members=members, start=start
                ),
                grid=(count,),
                in_specs=[VMEM] * len(operands),
                out_specs=[VMEM, VMEM],
                scratch_shapes=[pltpu.VMEM((heads, DH, DH), F32)],
                out_shape=[jax.ShapeDtypeStruct((blocks, width_in, NEAR), BF16), token],
                input_output_aliases=aliases,
                compiler_params=params(8),
                name="window",
            )(*operands)

        near, windows = None, None
        plane = seq_count // 4
        state = {"a": state_a, "b": state_b}
        received = []
        for half in "ab":
            received.append(exchanged(0, state[half]))
        target = [(i + plane) % seq_count if i % plane == plane - 1 else i for i in range(seq_count)]
        ahead_rim = lax.ppermute(rim, "seq", list(enumerate(target)))
        for level in range(levels - 1):
            if level == 2:
                picked = pl.pallas_call(
                    functools.partial(pick_kernel, plane=plane),
                    in_specs=[VMEM, VMEM],
                    out_specs=VMEM,
                    out_shape=jax.ShapeDtypeStruct(rim.shape, BF16),
                    compiler_params=params(4),
                    name="pick",
                )(rim, ahead_rim)
                target = [i // plane * plane + (i + 1) % plane for i in range(seq_count)]
                rim = lax.ppermute(picked, "seq", list(enumerate(target)))
            for half in "ab":
                step = COVERS.get((half, level))
                cover = []
                if step is not None:
                    kind, start, count = step
                    if kind == "near":
                        near, held = neared(start, count, near)
                    else:
                        windows, held = windowed(start, count, None, windows)
                    cover = [held]
                arrived = received[2 * level + "ab".index(half)]
                state[half] = joined(level, state[half], arrived, cover)
                received.append(exchanged(level + 1, state[half]))
        windows, _ = windowed(0, 1, [rim], windows)
        near = pl.pallas_call(
            far_kernel,
            grid=(blocks,),
            in_specs=[VMEM] * (2 + 2 * levels),
            out_specs=VMEM,
            out_shape=jax.ShapeDtypeStruct(near.shape, F32),
            input_output_aliases={3: 0},
            compiler_params=params(8),
            name="far",
        )(flags, weights, queries, near, *received[:-2])

        pieces = tokens // head_count // NEAR
        width = w_out.shape[1]
        shared = [flags, weights, queries, near, windows]
        shared += [gain_linear.reshape(heads, 1, DH), *received[-2:]]
        specs = [VMEM] * 8

        arrived = [[] for _ in range(pieces)]
        for away in range(1, head_count):
            route = [(i, (i + away) % head_count) for i in range(head_count)]
            for piece in range(pieces):
                partial = pl.pallas_call(
                    functools.partial(
                        partial_kernel, away=away, head_count=head_count, pieces=pieces, piece=piece
                    ),
                    in_specs=specs + [VMEM],
                    out_specs=VMEM,
                    out_shape=jax.ShapeDtypeStruct((NEAR, width), BF16),
                    compiler_params=params(8),
                    name="partial",
                )(*shared, w_out)
                arrived[piece].append(lax.ppermute(partial, "head", route))
        finished = []
        for piece in range(pieces - 1):
            attended = pl.pallas_call(
                functools.partial(attend_kernel, head_count=head_count, pieces=pieces, piece=piece),
                in_specs=specs,
                out_specs=VMEM,
                out_shape=jax.ShapeDtypeStruct((NEAR, width_in), BF16),
                compiler_params=params(8),
                name="attend",
            )(*shared)
            finished.append(
                pl.pallas_call(
                    project_kernel,
                    in_specs=[VMEM] * (2 + len(arrived[piece])),
                    out_specs=VMEM,
                    out_shape=jax.ShapeDtypeStruct((NEAR, width), BF16),
                    compiler_params=params(8),
                    name="project",
                )(attended, w_out, *arrived[piece])
            )
        others = len(arrived[-1])
        parts = 4
        return pl.pallas_call(
            functools.partial(last_kernel, head_count=head_count, pieces=pieces, others=others),
            in_specs=specs + [VMEM] * (others + pieces),
            out_specs=HELD,
            out_shape=jax.ShapeDtypeStruct((pieces * NEAR, width), BF16),
            scratch_shapes=[
                pltpu.VMEM((NEAR, width), BF16),
                pltpu.SemaphoreType.DMA((pieces - 1 + parts,)),
            ],
            compiler_params=params(8),
            name="last",
        )(*shared, w_out, *arrived[-1], *finished)

    return layer


def solution(mesh):
    placed = (
        P("seq", "head"),
        P("seq", "head"),
        P("seq", "head"),
        P("seq", "head"),
        P("seq", "head"),
        P(None, "seq"),
        P(None, "head"),
        P(),
        P("head"),
        P("head"),
        P("head", None),
    )
    return jax.shard_map(
        make_shards(mesh.shape["seq"], mesh.shape["head"]),
        mesh=mesh,
        in_specs=placed,
        out_specs=P(("seq", "head"), None),
        check_vma=False,
    )
```

```python
import functools

import jax
import jax.numpy as jnp
from jax import lax
from jax.experimental import pallas as pl
from jax.experimental.pallas import tpu as pltpu
from jax.sharding import PartitionSpec as P

DH = 128
WINDOW = 256
NEAR = 256
TILE = 128
GROUP = 8
EPSILON = 1e-06
LOG2_E = 1.4426950408889634
MEGABYTE = 1 << 20
BF16 = jnp.bfloat16
F32 = jnp.float32


def dot(a, b):
    return lax.dot_general(a, b, (((1,), (0,)), ((), ())), preferred_element_type=F32)


def dot_nt(a, b):
    return lax.dot_general(a, b, (((1,), (1,)), ((), ())), preferred_element_type=F32)


def local_spans(tokens):
    spans = []
    span = 1
    while span < tokens // NEAR:
        spans.append(span)
        span *= 2
    return spans


def local_buckets(tokens):
    blocks = tokens // NEAR
    return [(span, group) for span in local_spans(tokens) for group in range(1, blocks // span, 2)]


def weight_rows(index, table_ref, head, first_level):
    rows = jnp.zeros(index.shape, F32)
    for k in range(table_ref.shape[0]):
        rows = jnp.where(index == k, table_ref[k, head], rows)
    level = lax.broadcasted_iota(jnp.int32, index.shape, 0) + first_level
    return rows * jnp.exp2(-0.5 * level.astype(F32))


def head_columns(h):
    return slice(h * DH, (h + 1) * DH)


def state_kernel(
    lengths_hbm,
    k_hbm,
    v_hbm,
    wk_hbm,
    wv_hbm,
    k_ref,
    v_ref,
    rim_ref,
    local_ref,
    total_a_ref,
    total_b_ref,
    flags_ref,
    states,
    lengths_ref,
    sems,
    rim_sems,
    lengths_sem,
    *,
    levels,
):
    blocks = states.shape[0]
    heads = k_ref.shape[1] // DH
    copies = []
    for b in range(blocks):
        rows = pl.ds(b * NEAR, NEAR)
        pair = [
            pltpu.make_async_copy(k_hbm.at[rows], k_ref.at[rows], sems.at[0, b]),
            pltpu.make_async_copy(v_hbm.at[rows], v_ref.at[rows], sems.at[1, b]),
        ]
        for copy in pair:
            copy.start()
        copies.append(pair)
    last_rows = pl.ds(wk_hbm.shape[0] - WINDOW, WINDOW)
    width = wk_hbm.shape[1]
    late = [
        pltpu.make_async_copy(wk_hbm.at[last_rows], rim_ref.at[:, pl.ds(0, width)], rim_sems.at[0]),
        pltpu.make_async_copy(wv_hbm.at[last_rows], rim_ref.at[:, pl.ds(width, width)], rim_sems.at[1]),
        pltpu.make_async_copy(lengths_hbm, lengths_ref, lengths_sem),
    ]
    for copy in late:
        copy.start()
    for b in range(blocks):
        rows = slice(b * NEAR, (b + 1) * NEAR)
        for copy in copies[b]:
            copy.wait()
        for h in range(heads):
            at = head_columns(h)
            states[b, at, :] = dot(v_ref[rows, at].T, k_ref[rows, at])
    for place, (span, group) in enumerate(local_buckets(blocks * NEAR)):
        members = [states[b] for b in range((group - 1) * span, group * span)]
        local_ref[place] = functools.reduce(jnp.add, members).astype(BF16)
    middle_row = total_a_ref.shape[0]
    for total_ref, rows in ((total_a_ref, slice(0, middle_row)), (total_b_ref, slice(middle_row, None))):
        members = [states[b, rows, :] for b in range(blocks)]
        total_ref[...] = functools.reduce(jnp.add, members).astype(BF16)

    for copy in late:
        copy.wait()
    shard = lax.axis_index("seq")
    starts = [jnp.int32(0)]
    for s in range(lengths_ref.shape[0] - 1):
        starts.append(starts[-1] + lengths_ref[s])

    def begin_of(index):
        begin = jnp.int32(0)
        for start in starts[1:]:
            begin = jnp.where(start <= index, start, begin)
        return begin

    begin = begin_of(shard)
    rows = []
    for level in range(levels):
        last = shard | ((2 << level) - 1)
        middle = last - (1 << level)
        joined = jnp.where(begin_of(last) <= middle, 1.0, 0.0)
        right = (shard & (1 << level)) != 0
        rows.append(jnp.where(right, 1.0, joined))
        rows.append(jnp.where(right, joined, 1.0))
        rows.append(jnp.where(right & (begin <= middle), 1.0, 0.0))
    rows.append(jnp.where(begin == shard, -1e30, 0.0))
    for i, value in enumerate(rows):
        flags_ref[i : i + 1, :] = jnp.full((1, flags_ref.shape[1]), value, F32)


def flag_row(flags_ref, level, kind):
    return flags_ref[3 * level + kind : 3 * level + kind + 1, :]


def join_kernel(flags_ref, own_ref, arrived_ref, *rest, level):
    columns = own_ref.shape[1]
    own = own_ref[...] * flag_row(flags_ref, level, 0)[:, :columns].astype(BF16)
    rest[-1][...] = own + arrived_ref[...] * flag_row(flags_ref, level, 1)[:, :columns].astype(BF16)


def tile_mixing(weights):
    shape = (GROUP, TILE)
    row = lax.broadcasted_iota(jnp.int32, shape, 0)
    lane = lax.broadcasted_iota(jnp.int32, shape, 1)
    inner_bits = GROUP.bit_length() - 1
    within = lane % GROUP
    differ = row ^ within
    inner = jnp.where(differ == 0, weights[0:1], 0.0)
    for bit in range(inner_bits):
        inner = jnp.where((differ >> bit == 1) & (row < within), weights[bit + 1 : bit + 2], inner)
    shape = (TILE // GROUP, TILE)
    row = lax.broadcasted_iota(jnp.int32, shape, 0)
    above = lax.broadcasted_iota(jnp.int32, shape, 1) // GROUP
    differ = row ^ above
    outer = jnp.zeros(shape, F32)
    for bit in range((TILE // GROUP).bit_length() - 1):
        level = inner_bits + 1 + bit
        outer = jnp.where((differ >> bit == 1) & (row < above), weights[level : level + 1], outer)
    pieces = [
        jnp.where(lane // GROUP == g, inner, jnp.broadcast_to(outer[g : g + 1], (GROUP, TILE)))
        for g in range(TILE // GROUP)
    ]
    return jnp.concatenate(pieces, axis=0)


def weights_kernel(table_ref, index_ref, weights_ref):
    for h in range(weights_ref.shape[0]):
        weights_ref[h] = weight_rows(index_ref[...], table_ref, h, 0)


def near_kernel(weights_ref, q_ref, k_ref, v_ref, local_ref, *rest, spans, start):
    out_ref, token_ref = rest[-2:]
    token_ref[...] = jnp.zeros(token_ref.shape, F32)
    block = start + pl.program_id(0)
    blocks, width, _ = out_ref.shape
    near_bits = NEAR.bit_length() - 1
    tokens = pl.ds(pl.multiple_of(block * NEAR, NEAR), NEAR)
    places, present = [], []
    first = 0
    for span in spans:
        group = block // span
        places.append(first + group // 2)
        present.append((group % 2).astype(F32))
        first += blocks // span // 2
    for h in range(width // DH):
        at = head_columns(h)
        weights = weights_ref[h, :, tokens]
        queries_t = q_ref[tokens, at].T
        scores = dot(k_ref[tokens, at], queries_t)
        low = scores[:TILE, :TILE] * tile_mixing(weights[:, :TILE])
        cross = scores[:TILE, TILE:] * weights[near_bits : near_bits + 1, TILE:]
        high = scores[TILE:, TILE:] * tile_mixing(weights[:, TILE:])
        lhs = [v_ref[tokens, at].T]
        rhs = [
            jnp.concatenate([low.astype(BF16), cross.astype(BF16)], axis=1),
            jnp.concatenate([jnp.zeros((TILE, TILE), BF16), high.astype(BF16)], axis=1),
        ]
        for i, place in enumerate(places):
            level = near_bits + 1 + i
            row = (weights[level : level + 1] * present[i]).astype(BF16)
            lhs.append(local_ref[place, at, :])
            rhs.append(queries_t * row)
        out_ref[block, at, :] = dot(jnp.concatenate(lhs, axis=1), jnp.concatenate(rhs, axis=0))


def gain_column(gain_ref, h):
    return jnp.broadcast_to(gain_ref[h], (DH, DH)).T


def pick_kernel(own_ref, ahead_ref, out_ref, *, plane):
    closes = lax.axis_index("seq") % plane == plane - 1
    out_ref[...] = jnp.where(closes, ahead_ref[...], own_ref[...])


def window_kernel(flags_ref, q_ref, k_ref, v_ref, gain_ref, *rest, has_rim, members, start):
    out_ref, token_ref, gains = rest[-3:]
    token_ref[...] = jnp.zeros(token_ref.shape, F32)
    block = start + pl.program_id(0)
    heads = q_ref.shape[1] // DH
    scale = LOG2_E * DH**-0.5

    @pl.when(pl.program_id(0) == 0)
    def _():
        for h in range(heads):
            gains[h] = gain_column(gain_ref, h)

    key_row = lax.broadcasted_iota(jnp.int32, (TILE, TILE), 0)
    query_lane = lax.broadcasted_iota(jnp.int32, (TILE, TILE), 1)
    causal = key_row <= query_lane
    lower = jnp.where(causal, 1.0, 0.0).astype(BF16)
    now = pl.multiple_of(block * NEAR, NEAR)
    if has_rim:
        bias = flags_ref[flags_ref.shape[0] - 1 :, :TILE]
    for g in range(heads // members):
        at = head_columns(g)
        if has_rim:
            old_k = rest[0][:, at]
            old_v = rest[0][:, head_columns(g + heads // members)]
        else:
            old_k = k_ref[pl.ds(now - WINDOW, WINDOW), at]
            old_v = v_ref[pl.ds(now - WINDOW, WINDOW), at]
        keys = jnp.concatenate([old_k, k_ref[pl.ds(now, NEAR), at]], axis=0)
        values_t = jnp.concatenate([old_v.T, v_ref[pl.ds(now, NEAR), at].T], axis=1)
        for h in range(g * members, (g + 1) * members):
            for tile in range(NEAR // TILE):
                queries = q_ref[pl.ds(now + tile * TILE, TILE), head_columns(h)]
                span = slice(tile * TILE, tile * TILE + WINDOW + TILE)
                scores = dot_nt(keys[span], queries)
                oldest, middle, newest = scores[:TILE], scores[TILE : 2 * TILE], scores[2 * TILE :]
                if has_rim:
                    oldest = oldest + bias
                    if tile == 0:
                        middle = middle + bias
                edge = jnp.where(causal, newest, oldest)
                peak = jnp.max(jnp.maximum(edge, middle), axis=0, keepdims=True)
                edge = jnp.exp2((edge - peak) * scale)
                middle = jnp.exp2((middle - peak) * scale)
                total = jnp.sum(edge + middle, axis=0, keepdims=True)
                edge = edge.astype(BF16)
                newest = edge * lower
                probs = jnp.concatenate([edge - newest, middle.astype(BF16), newest], axis=0)
                raw = dot(values_t[:, span], probs)
                mean = jnp.sum(raw * raw, axis=0, keepdims=True) * (1.0 / DH)
                scaled = raw * lax.rsqrt(mean + EPSILON * total * total) * gains[h]
                out_ref[block, head_columns(h), tile * TILE : (tile + 1) * TILE] = scaled.astype(BF16)


def far_terms(block, first, h, flags_ref, weights_ref, q_ref, bucket_refs):
    above = weights_ref.shape[1] - flags_ref.shape[0] // 3 + first
    tokens = pl.ds(pl.multiple_of(block * NEAR, NEAR), NEAR)
    queries_t = q_ref[tokens, head_columns(h)].T
    half = q_ref.shape[1] // 2 // DH
    lhs, rhs = [], []
    for i in range(len(bucket_refs) // 2):
        level = slice(above + i, above + i + 1)
        row = weights_ref[h, level, tokens] * flag_row(flags_ref, first + i, 2)
        lhs.append(bucket_refs[2 * i + h // half][head_columns(h % half), :])
        rhs.append(queries_t * row.astype(BF16))
    return dot(jnp.concatenate(lhs, axis=1), jnp.concatenate(rhs, axis=0))


def far_kernel(flags_ref, weights_ref, q_ref, near_ref, *rest):
    bucket_refs, out_ref = rest[:-1], rest[-1]
    block = pl.program_id(0)
    for h in range(q_ref.shape[1] // DH):
        at = head_columns(h)
        reached = far_terms(block, 0, h, flags_ref, weights_ref, q_ref, bucket_refs)
        out_ref[block, at, :] = near_ref[block, at, :] + reached


def attend_head(block, h, flags_ref, weights_ref, q_ref, near_ref, win_ref, gain_ref, *bucket_refs):
    last = flags_ref.shape[0] // 3 - 1
    at = head_columns(h)
    reached = far_terms(block, last, h, flags_ref, weights_ref, q_ref, bucket_refs)
    total = near_ref[block, at, :] + reached
    mean = jnp.sum(total * total, axis=0, keepdims=True) * (1.0 / DH)
    gain = gain_column(gain_ref, h)
    gain = jnp.concatenate([gain] * (NEAR // DH), axis=1)
    total = total * lax.rsqrt(mean + EPSILON) * gain
    return (total + win_ref[block, at, :].astype(F32)).astype(BF16).T


def stage_kernel(*refs, head_count, pieces, now, after, carries):
    shared, w_ref = refs[:8], refs[8]
    heads = shared[2].shape[1] // DH

    def block_of(stage):
        away, piece = stage
        return lax.rem(lax.axis_index("head") + away, head_count) * pieces + piece

    if carries:
        attended = refs[9][...]
    else:
        attended = [attend_head(block_of(now), h, *shared) for h in range(heads)]
        attended = jnp.concatenate(attended, axis=1)
    out_ref = refs[-1] if after is None else refs[-2]
    step = w_ref.shape[1] // heads
    for h in range(heads):
        columns = slice(h * step, (h + 1) * step)
        out_ref[:, columns] = dot(attended, w_ref[:, columns]).astype(out_ref.dtype)
        if after is not None:
            refs[-1][:, head_columns(h)] = attend_head(block_of(after), h, *shared)


def finish_kernel(*refs, pieces):
    out_ref, result, sems = refs[-3:]
    copies = []
    for piece in range(pieces):
        parts = refs[piece:-3:pieces]
        for row in range(0, NEAR, TILE):
            rows = slice(row, row + TILE)
            total = parts[0][rows, :]
            for part in parts[1:]:
                total = total + part[rows, :].astype(F32)
            at = pl.ds(piece * NEAR + row, TILE)
            result[piece * NEAR + row : piece * NEAR + row + TILE, :] = total.astype(BF16)
            copies.append(pltpu.make_async_copy(result.at[at], out_ref.at[at], sems.at[len(copies)]))
            copies[-1].start()
    for copy in copies:
        copy.wait()


def in_hbm(array):
    return pltpu.with_memory_space_constraint(array, pltpu.HBM)


SMEM = pl.BlockSpec(memory_space=pltpu.SMEM)
VMEM = pl.BlockSpec(memory_space=pltpu.VMEM)
HELD = pl.BlockSpec(memory_space=pl.ANY)


COVERS = {
    ("a", 0): ("near", 0, 2),
    ("b", 0): ("near", 2, 1),
    ("a", 1): ("near", 3, 1),
    ("b", 1): ("window", 1, 1),
    ("a", 2): ("window", 2, 1),
    ("b", 2): ("window", 3, 1),
}


def make_shards(seq_count, head_count):
    def layer(
        queries,
        lin_keys,
        lin_values,
        window_keys,
        window_values,
        level_index,
        level_table,
        seq_lengths,
        gain_linear,
        gain_window,
        w_out,
    ):
        tokens, width_in = queries.shape
        heads = level_table.shape[1]
        groups = window_keys.shape[1] // DH
        members = heads // groups
        levels = seq_count.bit_length() - 1
        blocks = tokens // NEAR
        buckets = len(local_buckets(tokens))

        def params(megabytes):
            return pltpu.CompilerParams(vmem_limit_bytes=megabytes * MEGABYTE)

        states_call = pl.pallas_call(
            functools.partial(state_kernel, levels=levels),
            in_specs=[HELD] * 5,
            out_specs=[VMEM] * 7,
            out_shape=[
                jax.ShapeDtypeStruct(lin_keys.shape, BF16),
                jax.ShapeDtypeStruct(lin_values.shape, BF16),
                jax.ShapeDtypeStruct((WINDOW, 2 * window_keys.shape[1]), BF16),
                jax.ShapeDtypeStruct((buckets, width_in, DH), BF16),
                jax.ShapeDtypeStruct((width_in // 2, DH), BF16),
                jax.ShapeDtypeStruct((width_in // 2, DH), BF16),
                jax.ShapeDtypeStruct((3 * levels + 1, NEAR), F32),
            ],
            scratch_shapes=[
                pltpu.VMEM((blocks, width_in, DH), F32),
                pltpu.SMEM(seq_lengths.shape, jnp.int32),
                pltpu.SemaphoreType.DMA((2, blocks)),
                pltpu.SemaphoreType.DMA((2,)),
                pltpu.SemaphoreType.DMA,
            ],
            compiler_params=params(16),
            name="states",
        )
        keys, values, rim, local_states, state_a, state_b, flags = states_call(
            *[in_hbm(a) for a in (seq_lengths, lin_keys, lin_values, window_keys, window_values)]
        )

        def exchanged(level, state):
            route = [(i, i ^ (1 << level)) for i in range(seq_count)]
            return lax.ppermute(state, "seq", route)

        def joined(level, state, arrived, cover):
            return pl.pallas_call(
                functools.partial(join_kernel, level=level),
                in_specs=[VMEM] * (3 + len(cover)),
                out_specs=VMEM,
                out_shape=jax.ShapeDtypeStruct(state.shape, BF16),
                compiler_params=params(4),
                name="join",
            )(flags, state, arrived, *cover)

        token = jax.ShapeDtypeStruct((GROUP, TILE), F32)
        weights = pl.pallas_call(
            weights_kernel,
            in_specs=[SMEM, VMEM],
            out_specs=VMEM,
            out_shape=jax.ShapeDtypeStruct((heads, *level_index.shape), F32),
            compiler_params=params(8),
            name="weights",
        )(level_table, level_index)

        def neared(start, count, base):
            operands = [weights, queries, keys, values, local_states]
            aliases = {}
            if base is not None:
                aliases = {len(operands): 0}
                operands.append(base)
            return pl.pallas_call(
                functools.partial(near_kernel, spans=local_spans(tokens), start=start),
                grid=(count,),
                in_specs=[VMEM] * len(operands),
                out_specs=[VMEM, VMEM],
                out_shape=[jax.ShapeDtypeStruct((blocks, width_in, NEAR), F32), token],
                input_output_aliases=aliases,
                compiler_params=params(8),
                name="near",
            )(*operands)

        window_gains = gain_window.reshape(heads, 1, DH)

        def windowed(start, count, rim, base):
            operands = [flags, queries, window_keys, window_values, window_gains]
            aliases = {}
            if rim is not None:
                operands += rim
            if base is not None:
                aliases = {len(operands): 0}
                operands.append(base)
            return pl.pallas_call(
                functools.partial(
                    window_kernel, has_rim=rim is not None, members=members, start=start
                ),
                grid=(count,),
                in_specs=[VMEM] * len(operands),
                out_specs=[VMEM, VMEM],
                scratch_shapes=[pltpu.VMEM((heads, DH, DH), F32)],
                out_shape=[jax.ShapeDtypeStruct((blocks, width_in, NEAR), BF16), token],
                input_output_aliases=aliases,
                compiler_params=params(8),
                name="window",
            )(*operands)

        near, windows = None, None
        plane = seq_count // 4
        state = {"a": state_a, "b": state_b}
        received = []
        for half in "ab":
            received.append(exchanged(0, state[half]))
        target = [(i + plane) % seq_count if i % plane == plane - 1 else i for i in range(seq_count)]
        ahead_rim = lax.ppermute(rim, "seq", list(enumerate(target)))
        for level in range(levels - 1):
            if level == 2:
                picked = pl.pallas_call(
                    functools.partial(pick_kernel, plane=plane),
                    in_specs=[VMEM, VMEM],
                    out_specs=VMEM,
                    out_shape=jax.ShapeDtypeStruct(rim.shape, BF16),
                    compiler_params=params(4),
                    name="pick",
                )(rim, ahead_rim)
                target = [i // plane * plane + (i + 1) % plane for i in range(seq_count)]
                rim = lax.ppermute(picked, "seq", list(enumerate(target)))
            for half in "ab":
                step = COVERS.get((half, level))
                cover = []
                if step is not None:
                    kind, start, count = step
                    if kind == "near":
                        near, held = neared(start, count, near)
                    else:
                        windows, held = windowed(start, count, None, windows)
                    cover = [held]
                arrived = received[2 * level + "ab".index(half)]
                state[half] = joined(level, state[half], arrived, cover)
                received.append(exchanged(level + 1, state[half]))
        windows, _ = windowed(0, 1, [rim], windows)
        near = pl.pallas_call(
            far_kernel,
            grid=(blocks,),
            in_specs=[VMEM] * (2 + 2 * levels),
            out_specs=VMEM,
            out_shape=jax.ShapeDtypeStruct(near.shape, F32),
            input_output_aliases={3: 0},
            compiler_params=params(8),
            name="far",
        )(flags, weights, queries, near, *received[:-2])

        pieces = tokens // head_count // NEAR
        width = w_out.shape[1]
        shared = [flags, weights, queries, near, windows]
        shared += [gain_linear.reshape(heads, 1, DH), *received[-2:]]
        specs = [VMEM] * 8

        stages = [(away, piece) for away in range(1, head_count) for piece in range(pieces)]
        stages += [(0, piece) for piece in range(pieces)]
        attended, arrived, own = None, [], []
        for i, (away, piece) in enumerate(stages):
            after = stages[i + 1] if i + 1 < len(stages) else None
            carried = [] if attended is None else [attended]
            shapes = [jax.ShapeDtypeStruct((NEAR, width), BF16 if away else F32)]
            if after is not None:
                shapes.append(jax.ShapeDtypeStruct((NEAR, width_in), BF16))
            product, *attended = pl.pallas_call(
                functools.partial(
                    stage_kernel,
                    head_count=head_count,
                    pieces=pieces,
                    now=(away, piece),
                    after=after,
                    carries=bool(carried),
                ),
                in_specs=specs + [VMEM] * (1 + len(carried)),
                out_specs=[VMEM] * len(shapes),
                out_shape=shapes,
                compiler_params=params(8),
                name="stage",
            )(*shared, w_out, *carried)
            attended = attended[0] if attended else None
            if away:
                route = [(i, (i + away) % head_count) for i in range(head_count)]
                arrived.append(lax.ppermute(product, "head", route))
            else:
                own.append(product)
        return pl.pallas_call(
            functools.partial(finish_kernel, pieces=pieces),
            in_specs=[VMEM] * (len(own) + len(arrived)),
            out_specs=HELD,
            out_shape=jax.ShapeDtypeStruct((pieces * NEAR, width), BF16),
            scratch_shapes=[
                pltpu.VMEM((pieces * NEAR, width), BF16),
                pltpu.SemaphoreType.DMA((pieces * (NEAR // TILE),)),
            ],
            compiler_params=params(8),
            name="finish",
        )(*own, *arrived)

    return layer


def solution(mesh):
    placed = (
        P("seq", "head"),
        P("seq", "head"),
        P("seq", "head"),
        P("seq", "head"),
        P("seq", "head"),
        P(None, "seq"),
        P(None, "head"),
        P(),
        P("head"),
        P("head"),
        P("head", None),
    )
    return jax.shard_map(
        make_shards(mesh.shape["seq"], mesh.shape["head"]),
        mesh=mesh,
        in_specs=placed,
        out_specs=P(("seq", "head"), None),
        check_vma=False,
    )
```

```python
import functools

import jax
import jax.numpy as jnp
from jax import lax
from jax.experimental import pallas as pl
from jax.experimental.pallas import tpu as pltpu
from jax.sharding import PartitionSpec as P

DH = 128
WINDOW = 256
NEAR = 256
TILE = 128
GROUP = 8
EPSILON = 1e-06
LOG2_E = 1.4426950408889634
MEGABYTE = 1 << 20
BF16 = jnp.bfloat16
F32 = jnp.float32


def dot(a, b):
    return lax.dot_general(a, b, (((1,), (0,)), ((), ())), preferred_element_type=F32)


def dot_nt(a, b):
    return lax.dot_general(a, b, (((1,), (1,)), ((), ())), preferred_element_type=F32)


def local_spans(tokens):
    spans = []
    span = 1
    while span < tokens // NEAR:
        spans.append(span)
        span *= 2
    return spans


def local_buckets(tokens):
    blocks = tokens // NEAR
    return [(span, group) for span in local_spans(tokens) for group in range(1, blocks // span, 2)]


def weight_rows(index, table_ref, head, first_level):
    rows = jnp.zeros(index.shape, F32)
    for k in range(table_ref.shape[0]):
        rows = jnp.where(index == k, table_ref[k, head], rows)
    level = lax.broadcasted_iota(jnp.int32, index.shape, 0) + first_level
    return rows * jnp.exp2(-0.5 * level.astype(F32))


def head_columns(h):
    return slice(h * DH, (h + 1) * DH)


def state_kernel(
    lengths_hbm,
    k_hbm,
    v_hbm,
    wk_hbm,
    wv_hbm,
    k_ref,
    v_ref,
    rim_ref,
    local_ref,
    total_a_ref,
    total_b_ref,
    flags_ref,
    states,
    lengths_ref,
    sems,
    rim_sems,
    lengths_sem,
    *,
    levels,
):
    blocks = states.shape[0]
    heads = k_ref.shape[1] // DH
    copies = []
    for b in range(blocks):
        rows = pl.ds(b * NEAR, NEAR)
        pair = [
            pltpu.make_async_copy(k_hbm.at[rows], k_ref.at[rows], sems.at[0, b]),
            pltpu.make_async_copy(v_hbm.at[rows], v_ref.at[rows], sems.at[1, b]),
        ]
        for copy in pair:
            copy.start()
        copies.append(pair)
    last_rows = pl.ds(wk_hbm.shape[0] - WINDOW, WINDOW)
    width = wk_hbm.shape[1]
    late = [
        pltpu.make_async_copy(wk_hbm.at[last_rows], rim_ref.at[:, pl.ds(0, width)], rim_sems.at[0]),
        pltpu.make_async_copy(wv_hbm.at[last_rows], rim_ref.at[:, pl.ds(width, width)], rim_sems.at[1]),
        pltpu.make_async_copy(lengths_hbm, lengths_ref, lengths_sem),
    ]
    for copy in late:
        copy.start()
    for b in range(blocks):
        rows = slice(b * NEAR, (b + 1) * NEAR)
        for copy in copies[b]:
            copy.wait()
        for h in range(heads):
            at = head_columns(h)
            states[b, at, :] = dot(v_ref[rows, at].T, k_ref[rows, at])
    for place, (span, group) in enumerate(local_buckets(blocks * NEAR)):
        members = [states[b] for b in range((group - 1) * span, group * span)]
        local_ref[place] = functools.reduce(jnp.add, members).astype(BF16)
    middle_row = total_a_ref.shape[0]
    for total_ref, rows in ((total_a_ref, slice(0, middle_row)), (total_b_ref, slice(middle_row, None))):
        members = [states[b, rows, :] for b in range(blocks)]
        total_ref[...] = functools.reduce(jnp.add, members).astype(BF16)

    for copy in late:
        copy.wait()
    shard = lax.axis_index("seq")
    starts = [jnp.int32(0)]
    for s in range(lengths_ref.shape[0] - 1):
        starts.append(starts[-1] + lengths_ref[s])

    def begin_of(index):
        begin = jnp.int32(0)
        for start in starts[1:]:
            begin = jnp.where(start <= index, start, begin)
        return begin

    begin = begin_of(shard)
    rows = []
    for level in range(levels):
        last = shard | ((2 << level) - 1)
        middle = last - (1 << level)
        joined = jnp.where(begin_of(last) <= middle, 1.0, 0.0)
        right = (shard & (1 << level)) != 0
        rows.append(jnp.where(right, 1.0, joined))
        rows.append(jnp.where(right, joined, 1.0))
        rows.append(jnp.where(right & (begin <= middle), 1.0, 0.0))
    rows.append(jnp.where(begin == shard, -1e30, 0.0))
    for i, value in enumerate(rows):
        flags_ref[i : i + 1, :] = jnp.full((1, flags_ref.shape[1]), value, F32)


def flag_row(flags_ref, level, kind):
    return flags_ref[3 * level + kind : 3 * level + kind + 1, :]


def join_kernel(flags_ref, own_ref, arrived_ref, *rest, level):
    columns = own_ref.shape[1]
    own = own_ref[...] * flag_row(flags_ref, level, 0)[:, :columns].astype(BF16)
    rest[-1][...] = own + arrived_ref[...] * flag_row(flags_ref, level, 1)[:, :columns].astype(BF16)


def tile_mixing(weights):
    shape = (GROUP, TILE)
    row = lax.broadcasted_iota(jnp.int32, shape, 0)
    lane = lax.broadcasted_iota(jnp.int32, shape, 1)
    inner_bits = GROUP.bit_length() - 1
    within = lane % GROUP
    differ = row ^ within
    inner = jnp.where(differ == 0, weights[0:1], 0.0)
    for bit in range(inner_bits):
        inner = jnp.where((differ >> bit == 1) & (row < within), weights[bit + 1 : bit + 2], inner)
    shape = (TILE // GROUP, TILE)
    row = lax.broadcasted_iota(jnp.int32, shape, 0)
    above = lax.broadcasted_iota(jnp.int32, shape, 1) // GROUP
    differ = row ^ above
    outer = jnp.zeros(shape, F32)
    for bit in range((TILE // GROUP).bit_length() - 1):
        level = inner_bits + 1 + bit
        outer = jnp.where((differ >> bit == 1) & (row < above), weights[level : level + 1], outer)
    pieces = [
        jnp.where(lane // GROUP == g, inner, jnp.broadcast_to(outer[g : g + 1], (GROUP, TILE)))
        for g in range(TILE // GROUP)
    ]
    return jnp.concatenate(pieces, axis=0)


def weights_kernel(table_ref, index_ref, weights_ref):
    for h in range(weights_ref.shape[0]):
        weights_ref[h] = weight_rows(index_ref[...], table_ref, h, 0)


def near_kernel(weights_ref, q_ref, k_ref, v_ref, local_ref, *rest, spans, start):
    out_ref, token_ref = rest[-2:]
    token_ref[...] = jnp.zeros(token_ref.shape, F32)
    block = start + pl.program_id(0)
    blocks, width, _ = out_ref.shape
    near_bits = NEAR.bit_length() - 1
    tokens = pl.ds(pl.multiple_of(block * NEAR, NEAR), NEAR)
    places, present = [], []
    first = 0
    for span in spans:
        group = block // span
        places.append(first + group // 2)
        present.append((group % 2).astype(F32))
        first += blocks // span // 2
    for h in range(width // DH):
        at = head_columns(h)
        weights = weights_ref[h, :, tokens]
        queries_t = q_ref[tokens, at].T
        scores = dot(k_ref[tokens, at], queries_t)
        low = scores[:TILE, :TILE] * tile_mixing(weights[:, :TILE])
        cross = scores[:TILE, TILE:] * weights[near_bits : near_bits + 1, TILE:]
        high = scores[TILE:, TILE:] * tile_mixing(weights[:, TILE:])
        lhs = [v_ref[tokens, at].T]
        rhs = [
            jnp.concatenate([low.astype(BF16), cross.astype(BF16)], axis=1),
            jnp.concatenate([jnp.zeros((TILE, TILE), BF16), high.astype(BF16)], axis=1),
        ]
        for i, place in enumerate(places):
            level = near_bits + 1 + i
            row = (weights[level : level + 1] * present[i]).astype(BF16)
            lhs.append(local_ref[place, at, :])
            rhs.append(queries_t * row)
        out_ref[block, at, :] = dot(jnp.concatenate(lhs, axis=1), jnp.concatenate(rhs, axis=0))


def gain_column(gain_ref, h):
    return jnp.broadcast_to(gain_ref[h], (DH, DH)).T


def pick_kernel(own_ref, ahead_ref, out_ref, *, plane):
    closes = lax.axis_index("seq") % plane == plane - 1
    out_ref[...] = jnp.where(closes, ahead_ref[...], own_ref[...])


def window_kernel(flags_ref, q_ref, k_ref, v_ref, gain_ref, *rest, has_rim, members, start):
    out_ref, token_ref, gains = rest[-3:]
    token_ref[...] = jnp.zeros(token_ref.shape, F32)
    block = start + pl.program_id(0)
    heads = q_ref.shape[1] // DH
    scale = LOG2_E * DH**-0.5

    @pl.when(pl.program_id(0) == 0)
    def _():
        for h in range(heads):
            gains[h] = gain_column(gain_ref, h)

    key_row = lax.broadcasted_iota(jnp.int32, (TILE, TILE), 0)
    query_lane = lax.broadcasted_iota(jnp.int32, (TILE, TILE), 1)
    causal = key_row <= query_lane
    lower = jnp.where(causal, 1.0, 0.0).astype(BF16)
    now = pl.multiple_of(block * NEAR, NEAR)
    if has_rim:
        bias = flags_ref[flags_ref.shape[0] - 1 :, :TILE]
    for g in range(heads // members):
        at = head_columns(g)
        if has_rim:
            old_k = rest[0][:, at]
            old_v = rest[0][:, head_columns(g + heads // members)]
        else:
            old_k = k_ref[pl.ds(now - WINDOW, WINDOW), at]
            old_v = v_ref[pl.ds(now - WINDOW, WINDOW), at]
        keys = jnp.concatenate([old_k, k_ref[pl.ds(now, NEAR), at]], axis=0)
        values_t = jnp.concatenate([old_v.T, v_ref[pl.ds(now, NEAR), at].T], axis=1)
        for h in range(g * members, (g + 1) * members):
            for tile in range(NEAR // TILE):
                queries = q_ref[pl.ds(now + tile * TILE, TILE), head_columns(h)]
                span = slice(tile * TILE, tile * TILE + WINDOW + TILE)
                scores = dot_nt(keys[span], queries)
                oldest, middle, newest = scores[:TILE], scores[TILE : 2 * TILE], scores[2 * TILE :]
                if has_rim:
                    oldest = oldest + bias
                    if tile == 0:
                        middle = middle + bias
                edge = jnp.where(causal, newest, oldest)
                peak = jnp.max(jnp.maximum(edge, middle), axis=0, keepdims=True)
                edge = jnp.exp2((edge - peak) * scale)
                middle = jnp.exp2((middle - peak) * scale)
                total = jnp.sum(edge + middle, axis=0, keepdims=True)
                edge = edge.astype(BF16)
                newest = edge * lower
                probs = jnp.concatenate([edge - newest, middle.astype(BF16), newest], axis=0)
                raw = dot(values_t[:, span], probs)
                mean = jnp.sum(raw * raw, axis=0, keepdims=True) * (1.0 / DH)
                scaled = raw * lax.rsqrt(mean + EPSILON * total * total) * gains[h]
                out_ref[block, head_columns(h), tile * TILE : (tile + 1) * TILE] = scaled.astype(BF16)


def far_terms(block, first, h, flags_ref, weights_ref, q_ref, bucket_refs):
    above = weights_ref.shape[1] - flags_ref.shape[0] // 3 + first
    tokens = pl.ds(pl.multiple_of(block * NEAR, NEAR), NEAR)
    queries_t = q_ref[tokens, head_columns(h)].T
    half = q_ref.shape[1] // 2 // DH
    lhs, rhs = [], []
    for i in range(len(bucket_refs) // 2):
        level = slice(above + i, above + i + 1)
        row = weights_ref[h, level, tokens] * flag_row(flags_ref, first + i, 2)
        lhs.append(bucket_refs[2 * i + h // half][head_columns(h % half), :])
        rhs.append(queries_t * row.astype(BF16))
    return dot(jnp.concatenate(lhs, axis=1), jnp.concatenate(rhs, axis=0))


def far_kernel(flags_ref, weights_ref, q_ref, gain_ref, near_ref, *rest):
    bucket_refs, (out_ref, asked_ref, gains_ref) = rest[:-3], rest[-3:]
    block = pl.program_id(0)
    heads = q_ref.shape[1] // DH
    last = flags_ref.shape[0] // 3 - 1
    level = weights_ref.shape[1] - 1
    tokens = pl.ds(pl.multiple_of(block * NEAR, NEAR), NEAR)

    @pl.when(block == 0)
    def _():
        for h in range(heads):
            gains_ref[h] = gain_column(gain_ref, h)

    for h in range(heads):
        at = head_columns(h)
        reached = far_terms(block, 0, h, flags_ref, weights_ref, q_ref, bucket_refs)
        out_ref[block, at, :] = near_ref[block, at, :] + reached
        row = weights_ref[h, level : level + 1, tokens] * flag_row(flags_ref, last, 2)
        asked_ref[block, at, :] = q_ref[tokens, at].T * row.astype(BF16)


def attend_head(block, h, asked_ref, near_ref, win_ref, gains_ref, *bucket_refs):
    at = head_columns(h)
    half = near_ref.shape[1] // 2 // DH
    reached = dot(bucket_refs[h // half][head_columns(h % half), :], asked_ref[block, at, :])
    total = near_ref[block, at, :] + reached
    mean = jnp.sum(total * total, axis=0, keepdims=True) * (1.0 / DH)
    gain = jnp.concatenate([gains_ref[h]] * (NEAR // DH), axis=1)
    total = total * lax.rsqrt(mean + EPSILON) * gain
    return (total + win_ref[block, at, :].astype(F32)).astype(BF16).T


def stage_kernel(*refs, head_count, pieces, now, after, carries):
    shared, w_ref = refs[:6], refs[6]
    heads = shared[1].shape[1] // DH

    def block_of(stage):
        away, piece = stage
        return lax.rem(lax.axis_index("head") + away, head_count) * pieces + piece

    if carries:
        attended = refs[7][...]
    else:
        attended = [attend_head(block_of(now), h, *shared) for h in range(heads)]
        attended = jnp.concatenate(attended, axis=1)
    out_ref = refs[-1] if after is None else refs[-2]
    step = w_ref.shape[1] // heads
    for h in range(heads):
        columns = slice(h * step, (h + 1) * step)
        out_ref[:, columns] = dot(attended, w_ref[:, columns]).astype(out_ref.dtype)
        if after is not None:
            refs[-1][:, head_columns(h)] = attend_head(block_of(after), h, *shared)


def finish_kernel(*refs, pieces):
    out_ref, result, sems = refs[-3:]
    copies = []
    for piece in range(pieces):
        parts = refs[piece:-3:pieces]
        for row in range(0, NEAR, TILE):
            rows = slice(row, row + TILE)
            total = parts[0][rows, :]
            for part in parts[1:]:
                total = total + part[rows, :].astype(F32)
            at = pl.ds(piece * NEAR + row, TILE)
            result[piece * NEAR + row : piece * NEAR + row + TILE, :] = total.astype(BF16)
            copies.append(pltpu.make_async_copy(result.at[at], out_ref.at[at], sems.at[len(copies)]))
            copies[-1].start()
    for copy in copies:
        copy.wait()


def in_hbm(array):
    return pltpu.with_memory_space_constraint(array, pltpu.HBM)


SMEM = pl.BlockSpec(memory_space=pltpu.SMEM)
VMEM = pl.BlockSpec(memory_space=pltpu.VMEM)
HELD = pl.BlockSpec(memory_space=pl.ANY)


COVERS = {
    ("a", 0): ("near", 0, 2),
    ("b", 0): ("near", 2, 1),
    ("a", 1): ("near", 3, 1),
    ("b", 1): ("window", 1, 1),
    ("a", 2): ("window", 2, 1),
    ("b", 2): ("window", 3, 1),
}


def make_shards(seq_count, head_count):
    def layer(
        queries,
        lin_keys,
        lin_values,
        window_keys,
        window_values,
        level_index,
        level_table,
        seq_lengths,
        gain_linear,
        gain_window,
        w_out,
    ):
        tokens, width_in = queries.shape
        heads = level_table.shape[1]
        groups = window_keys.shape[1] // DH
        members = heads // groups
        levels = seq_count.bit_length() - 1
        blocks = tokens // NEAR
        buckets = len(local_buckets(tokens))

        def params(megabytes):
            return pltpu.CompilerParams(vmem_limit_bytes=megabytes * MEGABYTE)

        states_call = pl.pallas_call(
            functools.partial(state_kernel, levels=levels),
            in_specs=[HELD] * 5,
            out_specs=[VMEM] * 7,
            out_shape=[
                jax.ShapeDtypeStruct(lin_keys.shape, BF16),
                jax.ShapeDtypeStruct(lin_values.shape, BF16),
                jax.ShapeDtypeStruct((WINDOW, 2 * window_keys.shape[1]), BF16),
                jax.ShapeDtypeStruct((buckets, width_in, DH), BF16),
                jax.ShapeDtypeStruct((width_in // 2, DH), BF16),
                jax.ShapeDtypeStruct((width_in // 2, DH), BF16),
                jax.ShapeDtypeStruct((3 * levels + 1, NEAR), F32),
            ],
            scratch_shapes=[
                pltpu.VMEM((blocks, width_in, DH), F32),
                pltpu.SMEM(seq_lengths.shape, jnp.int32),
                pltpu.SemaphoreType.DMA((2, blocks)),
                pltpu.SemaphoreType.DMA((2,)),
                pltpu.SemaphoreType.DMA,
            ],
            compiler_params=params(16),
            name="states",
        )
        keys, values, rim, local_states, state_a, state_b, flags = states_call(
            *[in_hbm(a) for a in (seq_lengths, lin_keys, lin_values, window_keys, window_values)]
        )

        def exchanged(level, state):
            route = [(i, i ^ (1 << level)) for i in range(seq_count)]
            return lax.ppermute(state, "seq", route)

        def joined(level, state, arrived, cover):
            return pl.pallas_call(
                functools.partial(join_kernel, level=level),
                in_specs=[VMEM] * (3 + len(cover)),
                out_specs=VMEM,
                out_shape=jax.ShapeDtypeStruct(state.shape, BF16),
                compiler_params=params(4),
                name="join",
            )(flags, state, arrived, *cover)

        token = jax.ShapeDtypeStruct((GROUP, TILE), F32)
        weights = pl.pallas_call(
            weights_kernel,
            in_specs=[SMEM, VMEM],
            out_specs=VMEM,
            out_shape=jax.ShapeDtypeStruct((heads, *level_index.shape), F32),
            compiler_params=params(8),
            name="weights",
        )(level_table, level_index)

        def neared(start, count, base):
            operands = [weights, queries, keys, values, local_states]
            aliases = {}
            if base is not None:
                aliases = {len(operands): 0}
                operands.append(base)
            return pl.pallas_call(
                functools.partial(near_kernel, spans=local_spans(tokens), start=start),
                grid=(count,),
                in_specs=[VMEM] * len(operands),
                out_specs=[VMEM, VMEM],
                out_shape=[jax.ShapeDtypeStruct((blocks, width_in, NEAR), F32), token],
                input_output_aliases=aliases,
                compiler_params=params(8),
                name="near",
            )(*operands)

        window_gains = gain_window.reshape(heads, 1, DH)

        def windowed(start, count, rim, base):
            operands = [flags, queries, window_keys, window_values, window_gains]
            aliases = {}
            if rim is not None:
                operands += rim
            if base is not None:
                aliases = {len(operands): 0}
                operands.append(base)
            return pl.pallas_call(
                functools.partial(
                    window_kernel, has_rim=rim is not None, members=members, start=start
                ),
                grid=(count,),
                in_specs=[VMEM] * len(operands),
                out_specs=[VMEM, VMEM],
                scratch_shapes=[pltpu.VMEM((heads, DH, DH), F32)],
                out_shape=[jax.ShapeDtypeStruct((blocks, width_in, NEAR), BF16), token],
                input_output_aliases=aliases,
                compiler_params=params(8),
                name="window",
            )(*operands)

        near, windows = None, None
        plane = seq_count // 4
        state = {"a": state_a, "b": state_b}
        received = []
        for half in "ab":
            received.append(exchanged(0, state[half]))
        target = [(i + plane) % seq_count if i % plane == plane - 1 else i for i in range(seq_count)]
        ahead_rim = lax.ppermute(rim, "seq", list(enumerate(target)))
        for level in range(levels - 1):
            if level == 2:
                picked = pl.pallas_call(
                    functools.partial(pick_kernel, plane=plane),
                    in_specs=[VMEM, VMEM],
                    out_specs=VMEM,
                    out_shape=jax.ShapeDtypeStruct(rim.shape, BF16),
                    compiler_params=params(4),
                    name="pick",
                )(rim, ahead_rim)
                target = [i // plane * plane + (i + 1) % plane for i in range(seq_count)]
                rim = lax.ppermute(picked, "seq", list(enumerate(target)))
            for half in "ab":
                step = COVERS.get((half, level))
                cover = []
                if step is not None:
                    kind, start, count = step
                    if kind == "near":
                        near, held = neared(start, count, near)
                    else:
                        windows, held = windowed(start, count, None, windows)
                    cover = [held]
                arrived = received[2 * level + "ab".index(half)]
                state[half] = joined(level, state[half], arrived, cover)
                received.append(exchanged(level + 1, state[half]))
        windows, _ = windowed(0, 1, [rim], windows)
        near, asked, gains = pl.pallas_call(
            far_kernel,
            grid=(blocks,),
            in_specs=[VMEM] * (3 + 2 * levels),
            out_specs=[VMEM] * 3,
            out_shape=[
                jax.ShapeDtypeStruct(near.shape, F32),
                jax.ShapeDtypeStruct(near.shape, BF16),
                jax.ShapeDtypeStruct((heads, DH, DH), F32),
            ],
            input_output_aliases={4: 0},
            compiler_params=params(8),
            name="far",
        )(flags, weights, queries, gain_linear.reshape(heads, 1, DH), near, *received[:-2])

        pieces = tokens // head_count // NEAR
        width = w_out.shape[1]
        shared = [asked, near, windows, gains, *received[-2:]]
        specs = [VMEM] * len(shared)

        stages = [(away, piece) for away in range(1, head_count) for piece in range(pieces)]
        stages += [(0, piece) for piece in range(pieces)]
        attended, arrived, own = None, [], []
        for i, (away, piece) in enumerate(stages):
            after = stages[i + 1] if i + 1 < len(stages) else None
            carried = [] if attended is None else [attended]
            shapes = [jax.ShapeDtypeStruct((NEAR, width), BF16 if away else F32)]
            if after is not None:
                shapes.append(jax.ShapeDtypeStruct((NEAR, width_in), BF16))
            product, *attended = pl.pallas_call(
                functools.partial(
                    stage_kernel,
                    head_count=head_count,
                    pieces=pieces,
                    now=(away, piece),
                    after=after,
                    carries=bool(carried),
                ),
                in_specs=specs + [VMEM] * (1 + len(carried)),
                out_specs=[VMEM] * len(shapes),
                out_shape=shapes,
                compiler_params=params(8),
                name="stage",
            )(*shared, w_out, *carried)
            attended = attended[0] if attended else None
            if away:
                route = [(i, (i + away) % head_count) for i in range(head_count)]
                arrived.append(lax.ppermute(product, "head", route))
            else:
                own.append(product)
        return pl.pallas_call(
            functools.partial(finish_kernel, pieces=pieces),
            in_specs=[VMEM] * (len(own) + len(arrived)),
            out_specs=HELD,
            out_shape=jax.ShapeDtypeStruct((pieces * NEAR, width), BF16),
            scratch_shapes=[
                pltpu.VMEM((pieces * NEAR, width), BF16),
                pltpu.SemaphoreType.DMA((pieces * (NEAR // TILE),)),
            ],
            compiler_params=params(8),
            name="finish",
        )(*own, *arrived)

    return layer


def solution(mesh):
    placed = (
        P("seq", "head"),
        P("seq", "head"),
        P("seq", "head"),
        P("seq", "head"),
        P("seq", "head"),
        P(None, "seq"),
        P(None, "head"),
        P(),
        P("head"),
        P("head"),
        P("head", None),
    )
    return jax.shard_map(
        make_shards(mesh.shape["seq"], mesh.shape["head"]),
        mesh=mesh,
        in_specs=placed,
        out_specs=P(("seq", "head"), None),
        check_vma=False,
    )
```
